256 devices in a mesh: tm: 32 (over z_hi, y, core), chan: 8 (over x, z_lo).
Axes of the slice: x: 4, y: 4, z: 8 (z_hi: 4, z_lo: 2; z = z_hi * 2 + z_lo), core: 2. Of those that a mesh axis runs over, the one named last changes fastest.
Arguments:
- clip_input: bfloat16 [512, 64, 256], P('chan', 'tm'), may hold values from -16 to 16, as said below
- lengths: int32 [16], replicated, may hold values from 1 to 16, 64 in all
- gamma_one: float32 [512], P('chan'), may hold values from 0.25 to 1.75
- beta_one: float32 [512], P('chan'), may hold values from -1.5 to 1.5
- w_one: bfloat16 [512, 27, 512], P('chan'), may hold values from -0.0546875 to 0.0546875
- bias_one: float32 [512], P('chan'), may hold values from -1.5 to 1.5
- gamma_two: float32 [512], P('chan'), may hold values from 0.25 to 1.75
- beta_two: float32 [512], P('chan'), may hold values from -1.5 to 1.5
- w_two: bfloat16 [512, 27, 512], P('chan'), may hold values from -0.0546875 to 0.0546875
- bias_two: float32 [512], P('chan'), may hold values from -1.5 to 1.5
Outputs:
- block_output: float32 [512, 64, 256], P('chan', 'tm')
The draws below stay inside these ranges and needn't reach their ends.
Inputs may be any that keep to these rules, and one draw needn't show every extreme that they name: `clip_input`: activations of order one. `lengths`: the 16 counts sum to 64; the longest is exactly 16.
All inputs are finite; a program needn't handle non-finite values.
Results may differ from the reference program's by a relative error of at most 0.0054.
Values may be sent and summed in bfloat16 or wider, within the bound.
No kernel may reach another device: no remote copies, remote signals or barrier semaphores. Data moves between devices by JAX's collectives and lax.ppermute only.
A program may use at most 128 MiB of HBM per device.

```python
import math
import jax
import jax.numpy as jnp
import numpy as np
from jax import lax

C = 512
GROUPS = 32
H = 16
W = 16
FRAMES = 64
NCLIP = 16
MOST = 16


def draw_clip_input(key, part):
    k_base, k_chan, k_frame = jax.random.split(key, 3)
    chan_scale = jnp.exp(jax.random.uniform(k_chan, (C, 1, 1), jnp.float32, math.log(0.5), math.log(2.0)))
    frame_scale = jnp.exp(jax.random.uniform(k_frame, (1, FRAMES, 1), jnp.float32, math.log(0.5), math.log(2.0)))
    base = jnp.clip(jax.random.normal(k_base, (C, FRAMES, H * W), jnp.float32), -4.0, 4.0)
    return (base * chan_scale * frame_scale).astype(jnp.bfloat16)


def block_levels(stream_key, shape, cuts, low, high):
    factor_of = 1.0
    for dim, parts in cuts:
        steps = jax.random.uniform(jax.random.fold_in(jax.random.fold_in(stream_key, 6), dim), (parts,), jnp.float32, low / len(cuts), high / len(cuts))
        factor_of = factor_of * jnp.repeat(jnp.exp(steps), shape[dim] // parts).reshape((-1,) + (1,) * (len(shape) - 1 - dim))
    return factor_of


def profile(number_of, total, limit, skew):
    weights = [(1 << 20) // math.isqrt(standing ** skew) + 1 for standing in range(2, number_of + 1)]
    surplus, given = total - limit - (number_of - 1), [1] * (number_of - 1)
    while surplus > 0:
        candidates = [i for i in range(number_of - 1) if given[i] < limit]
        whole, budget = sum([weights[i] for i in candidates]), surplus
        for i in candidates:
            extra = min(limit - given[i], max(1, budget * weights[i] // whole), surplus)
            given[i] = given[i] + extra
            surplus = surplus - extra
    return np.array([limit] + given)


def ragged(own_key, amount, total, reach, lean):
    if amount == 2:
        one = jax.random.randint(own_key, (), max(1, total - reach), min(reach, total - 1) + 1)
        return jnp.stack([one, total - one])
    sizes = jnp.asarray(profile(amount, total, reach, lean), jnp.int32)
    twos = (amount - 1) // 2
    source_of, sink = sizes[1:1 + 2 * twos:2], sizes[2:2 + 2 * twos:2]
    slack = jnp.minimum(source_of - 1, reach - sink)
    moved = jax.random.randint(jax.random.fold_in(own_key, 1), (twos,), 0, 1 << 20) % (slack + 1)
    sizes = sizes.at[1:1 + 2 * twos:2].set(source_of - moved).at[2:2 + 2 * twos:2].set(sink + moved)
    return sizes[jax.random.permutation(jax.random.fold_in(own_key, 2), amount)]


def centred(key, extent, width, limit, cuts=(), held_as=jnp.bfloat16):
    level = block_levels(key, extent, cuts, -0.22, 0.18) if cuts else 1.0
    entries = jax.random.normal(key, extent, jnp.float32) * width * level
    return jnp.minimum(jnp.maximum(entries, -limit), limit).astype(held_as)


def setup_inputs(seed: int = 0) -> dict:
    keys = jax.random.split(jax.random.key(seed), 11)
    clip_input = draw_clip_input(jax.random.fold_in(keys[10], 71), 0)
    lengths = ragged(keys[1], NCLIP, FRAMES, MOST, 2).astype(jnp.int32)
    gamma_one = jnp.clip(1.0 + 0.15 * jax.random.normal(keys[2], (C,), jnp.float32), 0.25, 1.75)
    beta_one = centred(keys[3], (C,), 0.3, 1.5, ((0, 8),), jnp.float32)
    w_one = centred(keys[4], (C, 27, C), (27 * C) ** -0.5, 0.0546875, ((0, 8),))
    bias_one = centred(keys[5], (C,), 0.3, 1.5, ((0, 8),), jnp.float32)
    gamma_two = jnp.clip(1.0 + 0.15 * jax.random.normal(keys[6], (C,), jnp.float32), 0.25, 1.75)
    beta_two = centred(keys[7], (C,), 0.3, 1.5, ((0, 8),), jnp.float32)
    w_two = centred(keys[8], (C, 27, C), (27 * C) ** -0.5, 0.0546875, ((0, 8),))
    bias_two = centred(keys[9], (C,), 0.3, 1.5, ((0, 8),), jnp.float32)
    return {"clip_input": clip_input, "lengths": lengths, "gamma_one": gamma_one, "beta_one": beta_one, "w_one": w_one, "bias_one": bias_one, "gamma_two": gamma_two, "beta_two": beta_two, "w_two": w_two, "bias_two": bias_two}


EPS = 1e-06

def clip_of(frames, ends):
    return lax.optimization_barrier(jnp.sum((frames[:, None] >= ends[None, :]).astype(jnp.int32), axis=1)).astype(jnp.int32)

def group_norm(data, gamma, beta, member, counts):
    chans, frames, cells = data.shape
    grouped = data.reshape(GROUPS, chans // GROUPS, frames, cells)
    sums = lax.optimization_barrier(jnp.sum(grouped, axis=(1, 3)))
    squares = lax.optimization_barrier(jnp.sum(grouped * grouped, axis=(1, 3)))
    clip_sum = jnp.dot(sums, member, precision=lax.Precision.HIGHEST)
    clip_sq = jnp.dot(squares, member, precision=lax.Precision.HIGHEST)
    mean = clip_sum / counts[None, :]
    var = clip_sq / counts[None, :] - mean * mean
    scale = lax.rsqrt(var + EPS)
    mean_f = jnp.dot(mean, member.T, precision=lax.Precision.HIGHEST)
    scale_f = jnp.dot(scale, member.T, precision=lax.Precision.HIGHEST)
    normed = (grouped - mean_f[:, None, :, None]) * scale_f[:, None, :, None]
    normed = normed.reshape(chans, frames, cells) * gamma[:, None, None] + beta[:, None, None]
    return jax.nn.silu(normed).astype(jnp.bfloat16)

def causal_conv(hidden, weight, bias, ends, starts):
    chans, frames, cells = hidden.shape
    padded = jnp.pad(hidden.reshape(chans, frames, H, W), ((0, 0), (0, 0), (1, 1), (1, 1)))
    flat_w = weight.reshape(chans * 27, weight.shape[2])

    def one_frame(g):
        clip = clip_of(g[None], ends)[0]
        first = starts[clip]
        pieces = []
        for kt in range(3):
            src = g - 2 + kt
            keep = (src >= first).astype(jnp.bfloat16)
            frame = lax.dynamic_index_in_dim(padded, jnp.maximum(src, 0).astype(jnp.int32), 1, keepdims=False) * keep
            for kh in range(3):
                for kw in range(3):
                    pieces.append(frame[:, kh:kh + H, kw:kw + W].reshape(chans, H * W))
        cols = jnp.stack(pieces, axis=1).reshape(chans * 27, H * W)
        return jnp.dot(flat_w.T, cols, preferred_element_type=jnp.float32)
    out = lax.map(one_frame, jnp.arange(frames, dtype=jnp.int32))
    return jnp.transpose(out, (1, 0, 2)) + bias[:, None, None]

def reference(clip_input, lengths, gamma_one, beta_one, w_one, bias_one, gamma_two, beta_two, w_two, bias_two):
    ends = jnp.cumsum(lengths).astype(jnp.int32)
    starts = (ends - lengths).astype(jnp.int32)
    clips = clip_of(jnp.arange(FRAMES, dtype=jnp.int32), ends)
    member = (clips[:, None] == jnp.arange(NCLIP, dtype=jnp.int32)[None, :]).astype(jnp.float32)
    counts = lengths.astype(jnp.float32) * float(C // GROUPS * H * W)
    data = clip_input.astype(jnp.float32)
    h_one = group_norm(data, gamma_one, beta_one, member, counts)
    y_one = causal_conv(h_one, w_one, bias_one, ends, starts).astype(jnp.bfloat16)
    h_two = group_norm(y_one.astype(jnp.float32), gamma_two, beta_two, member, counts)
    y_two = causal_conv(h_two, w_two, bias_two, ends, starts)
    return data + y_two
```

```python
import jax
import jax.numpy as jnp
from jax import lax
from jax.sharding import PartitionSpec as P

C = 512
GROUPS = 32
H = 16
W = 16
EPS = 1e-06
GROUP_SIZE = C // GROUPS


def ring_shift(value, axis, steps):
    count = lax.axis_size(axis)
    return lax.ppermute(value, axis, [(source, (source + steps) % count) for source in range(count)])


def frame_sums(data):
    chans, frames, cells = data.shape
    grouped = data.reshape(chans // GROUP_SIZE, GROUP_SIZE, frames, cells)
    sums = jnp.sum(grouped, axis=(1, 3))
    squares = jnp.sum(grouped * grouped, axis=(1, 3))
    return jnp.stack([sums, squares], axis=0)


def share_over_clips(stats):
    count = lax.axis_size("tm")
    width = stats.size
    sent = jnp.broadcast_to(stats.reshape(1, width), (count, width))
    got = lax.all_to_all(sent, "tm", 0, 0, tiled=True)
    return jnp.moveaxis(got.reshape((count,) + stats.shape), 0, 2)


def conv_taps(weight_rows, extended, keep):
    rows, span, cells = extended.shape
    count = span - 2
    padded = jnp.pad(extended.reshape(rows, span, H, W), ((0, 0), (0, 0), (1, 1), (1, 1)))
    total = None
    for kt in range(3):
        for kh in range(3):
            for kw in range(3):
                piece = (
                    padded[:, kt : kt + count, kh : kh + H, kw : kw + W]
                    * keep[kt][None, :, None, None]
                )
                term = lax.dot_general(
                    weight_rows[:, 9 * kt + 3 * kh + kw, :],
                    piece.reshape(rows, count * H * W),
                    (((0,), (0,)), ((), ())),
                    preferred_element_type=jnp.float32,
                )
                total = term if total is None else total + term
    return total


def block_layer(raw, gamma, beta, weight, bias, same_clip, counts, keep):
    chans, frames, cells = raw.shape
    tail = ring_shift(raw, "tm", 1)
    stats = share_over_clips(frame_sums(raw.astype(jnp.float32)))
    stats = stats.reshape(2, chans // GROUP_SIZE, -1)
    clip = jnp.sum(stats[:, :, None, :] * same_clip[None, None], axis=3) / counts[None, None, :]
    mean = clip[0]
    scale = lax.rsqrt(clip[1] - mean * mean + EPS)
    mean = jnp.repeat(jnp.concatenate([mean[:, :1], mean[:, :1], mean], axis=1), GROUP_SIZE, axis=0)
    scale = jnp.repeat(jnp.concatenate([scale[:, :1], scale[:, :1], scale], axis=1), GROUP_SIZE, axis=0)
    data = jnp.concatenate([tail, raw], axis=1).astype(jnp.float32)
    normed = (data - mean[:, :, None]) * (scale * gamma[:, None])[:, :, None] + beta[:, None, None]
    extended = jax.nn.silu(normed).astype(jnp.bfloat16)
    partial = conv_taps(weight, extended, keep).astype(jnp.bfloat16)
    got = lax.all_to_all(partial, "chan", 0, 0, tiled=True)
    summed = jnp.sum(got.reshape(-1, chans, frames, cells).astype(jnp.float32), axis=0)
    return summed + bias[:, None, None]


def on_device(
    clip_input, lengths, gamma_one, beta_one, w_one, bias_one, gamma_two, beta_two, w_two, bias_two
):
    chans, frames, cells = clip_input.shape
    all_frames = frames * lax.axis_size("tm")
    ends = jnp.cumsum(lengths)
    starts = ends - lengths
    own = lax.axis_index("tm") * frames + jnp.arange(frames, dtype=jnp.int32)
    inside = ((own[:, None] >= starts[None, :]) & (own[:, None] < ends[None, :])).astype(jnp.int32)
    start = jnp.sum(inside * starts[None, :], axis=1)
    end = jnp.sum(inside * ends[None, :], axis=1)
    every = jnp.arange(all_frames, dtype=jnp.int32)
    same_clip = ((every[None, :] >= start[:, None]) & (every[None, :] < end[:, None])).astype(jnp.float32)
    counts = (end - start).astype(jnp.float32) * float(GROUP_SIZE * H * W)
    keep = jnp.stack([own - 2 + kt >= start for kt in range(3)], axis=0).astype(jnp.bfloat16)
    y_one = block_layer(clip_input, gamma_one, beta_one, w_one, bias_one, same_clip, counts, keep)
    y_one = y_one.astype(jnp.bfloat16)
    y_two = block_layer(y_one, gamma_two, beta_two, w_two, bias_two, same_clip, counts, keep)
    return clip_input.astype(jnp.float32) + y_two


def solution(mesh):
    in_specs = (
        P("chan", "tm", None),
        P(),
        P("chan"),
        P("chan"),
        P("chan", None, None),
        P("chan"),
        P("chan"),
        P("chan"),
        P("chan", None, None),
        P("chan"),
    )
    out_specs = P("chan", "tm", None)
    return jax.shard_map(
        on_device, mesh=mesh, in_specs=in_specs, out_specs=out_specs, check_vma=False
    )
```

```python
import jax
import jax.numpy as jnp
from jax import lax
from jax.experimental import pallas as pl
from jax.experimental.pallas import tpu as pltpu
from jax.sharding import PartitionSpec as P

C = 512
GROUPS = 32
H = 16
W = 16
EPS = 1e-06
GROUP_SIZE = C // GROUPS
CELLS = H * W
CHANS = 64
LANES = 2 * CHANS
TAPS = 27
ROWS = TAPS * CHANS
DEPTH = (TAPS + 1) * CHANS
SLOT = CELLS + 2 * W

VMEM = pl.BlockSpec(memory_space=pltpu.VMEM)
SMEM = pl.BlockSpec(memory_space=pltpu.SMEM)
ANY = pl.BlockSpec(memory_space=pl.ANY)


def ring_shift(value, axis, steps):
    count = lax.axis_size(axis)
    return lax.ppermute(value, axis, [(source, (source + steps) % count) for source in range(count)])


def left_half(shape):
    return lax.broadcasted_iota(jnp.int32, shape, len(shape) - 1) < CHANS


def write_sums(values, sums_ref):
    total = jnp.sum(values, axis=0, keepdims=True)
    squares = jnp.sum(values * values, axis=0, keepdims=True)
    row = lax.broadcasted_iota(jnp.int32, (8, LANES), 0)
    tile = jnp.where(row == 0, total, jnp.where(row == 1, squares, 0.0))
    sums_ref[...] = jnp.broadcast_to(tile[None], sums_ref.shape)


def both_halves(row):
    return jnp.concatenate([row, row], axis=1)


def pack_kernel(x_ref, packed_ref, sums_ref):
    rows = jnp.concatenate([x_ref[:, 0, :], x_ref[:, 1, :]], axis=0).astype(jnp.float32)
    values = rows.T
    packed_ref[...] = values.astype(jnp.bfloat16)
    write_sums(values, sums_ref)


def group_totals(rows):
    lane = lax.broadcasted_iota(jnp.int32, rows.shape, 1)
    rows = rows + pltpu.roll(rows, CHANS, 1)
    step = 1
    while step < GROUP_SIZE:
        other = jnp.where(
            (lane & step) == 0, pltpu.roll(rows, LANES - step, 1), pltpu.roll(rows, step, 1)
        )
        rows = rows + other
        step *= 2
    return rows


def clip_bounds(lengths_ref, frame):
    total = jnp.int32(0)
    start = jnp.int32(0)
    end = jnp.int32(0)
    for k in range(lengths_ref.shape[0]):
        after = total + lengths_ref[k]
        inside = (frame >= total) & (frame < after)
        start = jnp.where(inside, total, start)
        end = jnp.where(inside, after, end)
        total = after
    return start, end


def conv_kernel(
    lengths_ref, first_ref, sums_ref, own_ref, tail_ref, gamma_ref, beta_ref, w_hbm, out_ref,
    w_ref, slots_ref, cols_ref, sem,
):
    load = pltpu.make_async_copy(w_hbm, w_ref.at[pl.ds(0, ROWS), :], sem)
    load.start()
    w_ref[ROWS:, :] = jnp.zeros((DEPTH - ROWS, C), jnp.bfloat16)

    frame = first_ref[0]
    bounds = [clip_bounds(lengths_ref, frame), clip_bounds(lengths_ref, frame + 1)]
    count = sums_ref.shape[0]
    device = lax.broadcasted_iota(jnp.int32, (count, 1, LANES), 0)
    half = (lax.broadcasted_iota(jnp.int32, (count, 1, LANES), 2) >= CHANS).astype(jnp.int32)
    frame_of = 2 * device + half
    sums = sums_ref[...]
    stats = []
    for start, end in bounds:
        inside = (frame_of >= start) & (frame_of < end)
        per_lane = jnp.sum(jnp.where(inside, sums, 0.0), axis=0)
        totals = group_totals(per_lane)
        size = ((end - start) * (GROUP_SIZE * CELLS)).astype(jnp.float32)
        totals = totals / size
        mean = totals[0:1, :]
        var = totals[1:2, :] - mean * mean
        stats.append((mean, lax.rsqrt(var + EPS)))
    gamma = both_halves(gamma_ref[...])
    beta = both_halves(beta_ref[...])
    left_row = left_half((1, LANES))
    mean_tail, scale_tail = stats[0]
    mean_own = jnp.where(left_row, stats[0][0], stats[1][0])
    scale_own = jnp.where(left_row, stats[0][1], stats[1][1])

    def normed(ref, mean, scale):
        u = (ref[...].astype(jnp.float32) - mean) * scale * gamma + beta
        return u / (1.0 + jnp.exp(-u))

    left = left_half((CELLS, LANES))

    def split(packed):
        turned = pltpu.roll(packed, CHANS, 1)
        return jnp.where(left, packed, turned), jnp.where(left, turned, packed)

    before_two, before_one = split(normed(tail_ref, mean_tail, scale_tail))
    own_zero, own_one = split(normed(own_ref, mean_own, scale_own))
    start_zero, start_one = bounds[0][0], bounds[1][0]
    column = lax.broadcasted_iota(jnp.int32, (CELLS, LANES), 0) % W
    margin = jnp.zeros((W, LANES), jnp.bfloat16)

    def place(kw, slot, value):
        slots_ref[kw, slot, 0:W, :] = margin
        slots_ref[kw, slot, W : W + CELLS, :] = value
        slots_ref[kw, slot, W + CELLS :, :] = margin

    uses = (
        (before_two, ((0, frame - 2 >= start_zero),)),
        (before_one, ((1, frame - 1 >= start_zero), (3, frame - 1 >= start_one))),
        (own_zero, ((2, None), (4, frame >= start_one))),
        (own_one, ((5, None),)),
    )
    for value, targets in uses:
        views = (
            jnp.where(column == 0, 0.0, pltpu.roll(value, 1, 0)),
            value,
            jnp.where(column == W - 1, 0.0, pltpu.roll(value, CELLS - 1, 0)),
        )
        for kw, view in enumerate(views):
            for slot, kept in targets:
                shown = view if kept is None else jnp.where(kept, view, 0.0)
                place(kw, slot, shown.astype(jnp.bfloat16))

    def tap(own, index):
        kt, kh, kw = index // 9, (index // 3) % 3, index % 3
        return slots_ref[kw, 3 * own + kt, kh * W : kh * W + CELLS, :]

    for own in range(2):
        for pair in range(DEPTH // LANES):
            first = tap(own, 2 * pair)
            second = tap(own, 2 * pair + 1) if 2 * pair + 1 < TAPS else jnp.zeros_like(first)
            cols_ref[own * CELLS : (own + 1) * CELLS, pair * LANES : (pair + 1) * LANES] = jnp.where(
                left, first, second
            )
    load.wait()
    for block in range(2):
        width = C // 2
        partial = jnp.dot(
            cols_ref[...],
            w_ref[:, block * width : (block + 1) * width],
            preferred_element_type=jnp.float32,
        )
        for tile in range(width // LANES):
            zero = partial[:CELLS, tile * LANES : (tile + 1) * LANES]
            one = partial[CELLS:, tile * LANES : (tile + 1) * LANES]
            place_at = block * (width // CHANS) + 2 * tile
            out_ref[place_at] = jnp.where(left, zero, pltpu.roll(one, CHANS, 1)).astype(jnp.bfloat16)
            out_ref[place_at + 1] = jnp.where(left, pltpu.roll(zero, CHANS, 1), one).astype(jnp.bfloat16)


def sum_partials(parts_ref, bias_ref):
    total = parts_ref[0].astype(jnp.float32)
    for k in range(1, parts_ref.shape[0]):
        total = total + parts_ref[k].astype(jnp.float32)
    return total + both_halves(bias_ref[...])


def middle_kernel(parts_ref, bias_ref, y_ref, sums_ref):
    y = sum_partials(parts_ref, bias_ref).astype(jnp.bfloat16)
    y_ref[...] = y
    write_sums(y.astype(jnp.float32), sums_ref)


def last_kernel(parts_ref, bias_ref, packed_ref, out_ref):
    value = sum_partials(parts_ref, bias_ref) + packed_ref[...].astype(jnp.float32)
    rows = value.T
    out_ref[:, 0, :] = rows[:CHANS]
    out_ref[:, 1, :] = rows[CHANS:]


def shape_of(shape, dtype):
    return jax.ShapeDtypeStruct(shape, dtype)


def normed_conv(packed, sums, lengths, first, gamma, beta, weight):
    tail = ring_shift(packed, "tm", 1)
    sums = lax.all_to_all(sums, "tm", 0, 0, tiled=True)
    parts = C // CHANS
    partial = pl.pallas_call(
        conv_kernel,
        out_shape=shape_of((parts, CELLS, LANES), jnp.bfloat16),
        in_specs=[SMEM, SMEM, VMEM, VMEM, VMEM, VMEM, VMEM, ANY],
        out_specs=VMEM,
        scratch_shapes=[
            pltpu.VMEM((DEPTH, C), jnp.bfloat16),
            pltpu.VMEM((3, 6, SLOT, LANES), jnp.bfloat16),
            pltpu.VMEM((2 * CELLS, DEPTH), jnp.bfloat16),
            pltpu.SemaphoreType.DMA,
        ],
        compiler_params=pltpu.CompilerParams(vmem_limit_bytes=24 << 20),
        cost_estimate=pl.CostEstimate(
            flops=2 * ROWS * C * 2 * CELLS, bytes_accessed=3 << 20, transcendentals=4 * CELLS * CHANS
        ),
        name="norm_conv",
    )(lengths, first, sums, packed, tail, gamma.reshape(1, CHANS), beta.reshape(1, CHANS), weight)
    return lax.all_to_all(partial, "chan", 0, 0, tiled=True)


def on_device(
    clip_input, lengths, gamma_one, beta_one, w_one, bias_one, gamma_two, beta_two, w_two, bias_two
):
    count = lax.axis_size("tm")
    first = (lax.axis_index("tm") * 2).astype(jnp.int32).reshape(1)
    packed_shape = shape_of((CELLS, LANES), jnp.bfloat16)
    sums_shape = shape_of((count, 8, LANES), jnp.float32)
    flat_one = jnp.transpose(w_one, (1, 0, 2)).reshape(ROWS, C)
    flat_two = jnp.transpose(w_two, (1, 0, 2)).reshape(ROWS, C)
    packed, sums = pl.pallas_call(
        pack_kernel,
        out_shape=(packed_shape, sums_shape),
        in_specs=[VMEM],
        out_specs=(VMEM, VMEM),
        name="pack",
    )(clip_input)
    parts = normed_conv(packed, sums, lengths, first, gamma_one, beta_one, flat_one)
    y_one, sums = pl.pallas_call(
        middle_kernel,
        out_shape=(packed_shape, sums_shape),
        in_specs=[VMEM, VMEM],
        out_specs=(VMEM, VMEM),
        name="middle",
    )(parts, bias_one.reshape(1, CHANS))
    parts = normed_conv(y_one, sums, lengths, first, gamma_two, beta_two, flat_two)
    return pl.pallas_call(
        last_kernel,
        out_shape=shape_of(clip_input.shape, jnp.float32),
        in_specs=[VMEM, VMEM, VMEM],
        out_specs=VMEM,
        name="last",
    )(parts, bias_two.reshape(1, CHANS), packed)


def solution(mesh):
    in_specs = (
        P("chan", "tm", None),
        P(),
        P("chan"),
        P("chan"),
        P("chan", None, None),
        P("chan"),
        P("chan"),
        P("chan"),
        P("chan", None, None),
        P("chan"),
    )
    out_specs = P("chan", "tm", None)
    return jax.shard_map(
        on_device, mesh=mesh, in_specs=in_specs, out_specs=out_specs, check_vma=False
    )
```

```python
import functools

import jax
import jax.numpy as jnp
from jax import lax
from jax.experimental import pallas as pl
from jax.experimental.pallas import tpu as pltpu
from jax.sharding import PartitionSpec as P

C = 512
GROUPS = 32
H = 16
W = 16
EPS = 1e-06
GROUP_SIZE = C // GROUPS
CELLS = H * W
CHANS = 64
LANES = 2 * CHANS
TAPS = 27
ROWS = TAPS * CHANS
DEPTH = (TAPS + 1) * CHANS
SLOT = CELLS + 2 * W

VMEM = pl.BlockSpec(memory_space=pltpu.VMEM)
SMEM = pl.BlockSpec(memory_space=pltpu.SMEM)
HBM = pl.BlockSpec(memory_space=pltpu.HBM)
SMALL = pltpu.CompilerParams(vmem_limit_bytes=4 << 20)


def ring_shift(value, axis, steps):
    count = lax.axis_size(axis)
    return lax.ppermute(value, axis, [(source, (source + steps) % count) for source in range(count)])


def left_half(shape):
    return lax.broadcasted_iota(jnp.int32, shape, len(shape) - 1) < CHANS


def group_totals(rows):
    lane = lax.broadcasted_iota(jnp.int32, rows.shape, 1)
    step = 1
    while step < GROUP_SIZE:
        other = jnp.where(
            (lane & step) == 0, pltpu.roll(rows, LANES - step, 1), pltpu.roll(rows, step, 1)
        )
        rows = rows + other
        step *= 2
    return rows


def holds_sum(shape):
    lane = lax.broadcasted_iota(jnp.int32, shape, len(shape) - 1)
    return (lane & (GROUP_SIZE // 2)) == 0


def write_sums(values, sums_ref):
    total = group_totals(jnp.sum(values, axis=0, keepdims=True))
    squares = group_totals(jnp.sum(values * values, axis=0, keepdims=True))
    row = jnp.where(holds_sum((1, LANES)), total, squares)
    sums_ref[...] = jnp.broadcast_to(row[None], sums_ref.shape)


def both_halves(row):
    return jnp.concatenate([row, row], axis=1)


def pack_kernel(x_hbm, packed_ref, sums_ref, x_ref, sem):
    load = pltpu.make_async_copy(x_hbm, x_ref, sem)
    load.start()
    load.wait()
    rows = jnp.concatenate([x_ref[:, 0, :], x_ref[:, 1, :]], axis=0).astype(jnp.float32)
    values = rows.T
    packed_ref[...] = values.astype(jnp.bfloat16)
    write_sums(values, sums_ref)


def clip_bounds(lengths_ref, frame):
    total = jnp.int32(0)
    start = jnp.int32(0)
    end = jnp.int32(0)
    for k in range(lengths_ref.shape[0]):
        after = total + lengths_ref[k]
        inside = (frame >= total) & (frame < after)
        start = jnp.where(inside, total, start)
        end = jnp.where(inside, after, end)
        total = after
    return start, end


def prepare_kernel(
    lengths_ref, first_ref, after_ref, weight_ref, affine_ref, params_ref, clips_ref
):
    del after_ref, weight_ref
    params_ref[...] = both_halves(affine_ref[...])
    frame = first_ref[0]
    start_zero, end_zero = clip_bounds(lengths_ref, frame)
    start_one, end_one = clip_bounds(lengths_ref, frame + 1)
    for k, number in enumerate((start_zero, end_zero, start_one, end_one, frame, frame, frame, frame)):
        clips_ref[k : k + 1, :] = jnp.full((1, LANES), number, jnp.int32)


def conv_kernel(
    at, sums_ref, own_ref, tail_ref, params_ref, clips_ref, w_ref, out_ref, slots_ref, cols_ref
):
    clips = clips_ref[...]
    start_zero, end_zero = clips[0:1, :], clips[1:2, :]
    start_one, end_one = clips[2:3, :], clips[3:4, :]
    frame = clips[4:5, :]
    count = sums_ref.shape[0]
    device = lax.broadcasted_iota(jnp.int32, (count, 1, LANES), 0)
    half = (lax.broadcasted_iota(jnp.int32, (count, 1, LANES), 2) >= CHANS).astype(jnp.int32)
    frame_of = 2 * device + half
    sums = sums_ref[...]
    is_sum = holds_sum((1, LANES))
    stats = []
    for start, end in ((start_zero, end_zero), (start_one, end_one)):
        inside = (frame_of >= start[None]) & (frame_of < end[None])
        row = jnp.sum(jnp.where(inside, sums, 0.0), axis=0)
        size = ((end - start) * (GROUP_SIZE * CELLS)).astype(jnp.float32)
        row = (row + pltpu.roll(row, CHANS, 1)) / size
        mean = jnp.where(is_sum, row, pltpu.roll(row, GROUP_SIZE // 2, 1))
        second = jnp.where(is_sum, pltpu.roll(row, LANES - GROUP_SIZE // 2, 1), row)
        stats.append((mean, lax.rsqrt(second - mean * mean + EPS)))
    gamma = params_ref[at : at + 1, :]
    beta = params_ref[at + 1 : at + 2, :]
    left_row = left_half((1, LANES))
    mean_tail, scale_tail = stats[0]
    mean_own = jnp.where(left_row, stats[0][0], stats[1][0])
    scale_own = jnp.where(left_row, stats[0][1], stats[1][1])

    def normed(ref, mean, scale):
        u = (ref[...].astype(jnp.float32) - mean) * scale * gamma + beta
        return u / (1.0 + jnp.exp(-u))

    left = left_half((CELLS, LANES))

    def split(packed):
        turned = pltpu.roll(packed, CHANS, 1)
        return jnp.where(left, packed, turned), jnp.where(left, turned, packed)

    before_two, before_one = split(normed(tail_ref, mean_tail, scale_tail))
    own_zero, own_one = split(normed(own_ref, mean_own, scale_own))
    column = lax.broadcasted_iota(jnp.int32, (CELLS, LANES), 0) % W
    margin = jnp.zeros((W, LANES), jnp.bfloat16)

    def place(kw, slot, value):
        slots_ref[kw, slot, 0:W, :] = margin
        slots_ref[kw, slot, W : W + CELLS, :] = value
        slots_ref[kw, slot, W + CELLS :, :] = margin

    uses = (
        (before_two, ((0, frame - 2 >= start_zero),)),
        (before_one, ((1, frame - 1 >= start_zero), (3, frame - 1 >= start_one))),
        (own_zero, ((2, None), (4, frame >= start_one))),
        (own_one, ((5, None),)),
    )
    for value, targets in uses:
        views = (
            jnp.where(column == 0, 0.0, pltpu.roll(value, 1, 0)),
            value,
            jnp.where(column == W - 1, 0.0, pltpu.roll(value, CELLS - 1, 0)),
        )
        for kw, view in enumerate(views):
            for slot, kept in targets:
                shown = view if kept is None else jnp.where(kept, view, 0.0)
                place(kw, slot, shown.astype(jnp.bfloat16))

    def tap(own, index):
        kt, kh, kw = index // 9, (index // 3) % 3, index % 3
        return slots_ref[kw, 3 * own + kt, kh * W : kh * W + CELLS, :]

    for own in range(2):
        for pair in range(DEPTH // LANES):
            first = tap(own, 2 * pair)
            second = tap(own, 2 * pair + 1) if 2 * pair + 1 < TAPS else jnp.zeros_like(first)
            cols_ref[own * CELLS : (own + 1) * CELLS, pair * LANES : (pair + 1) * LANES] = jnp.where(
                left, first, second
            )
    for block in range(2):
        width = C // 2
        partial = jnp.dot(
            cols_ref[:, :ROWS],
            w_ref[:, block * width : (block + 1) * width],
            preferred_element_type=jnp.float32,
        )
        for tile in range(width // LANES):
            zero = partial[:CELLS, tile * LANES : (tile + 1) * LANES]
            one = partial[CELLS:, tile * LANES : (tile + 1) * LANES]
            place_at = block * (width // CHANS) + 2 * tile
            out_ref[place_at] = jnp.where(left, zero, pltpu.roll(one, CHANS, 1)).astype(jnp.bfloat16)
            out_ref[place_at + 1] = jnp.where(left, pltpu.roll(zero, CHANS, 1), one).astype(jnp.bfloat16)


def sum_partials(parts_ref, bias):
    total = parts_ref[0].astype(jnp.float32)
    for k in range(1, parts_ref.shape[0]):
        total = total + parts_ref[k].astype(jnp.float32)
    return total + bias


def middle_kernel(parts_ref, params_ref, y_ref, sums_ref):
    y = sum_partials(parts_ref, params_ref[2:3, :]).astype(jnp.bfloat16)
    y_ref[...] = y
    write_sums(y.astype(jnp.float32), sums_ref)


def last_kernel(parts_ref, params_ref, packed_ref, out_ref):
    value = sum_partials(parts_ref, params_ref[5:6, :]) + packed_ref[...].astype(jnp.float32)
    rows = value.T
    out_ref[:, 0, :] = rows[:CHANS]
    out_ref[:, 1, :] = rows[CHANS:]


def shape_of(shape, dtype):
    return jax.ShapeDtypeStruct(shape, dtype)


def normed_conv(at, tail, packed, sums, params, clips, weight):
    parts = C // CHANS
    partial = pl.pallas_call(
        functools.partial(conv_kernel, at),
        out_shape=shape_of((parts, CELLS, LANES), jnp.bfloat16),
        in_specs=[VMEM, VMEM, VMEM, VMEM, VMEM, VMEM],
        out_specs=VMEM,
        scratch_shapes=[
            pltpu.VMEM((3, 6, SLOT, LANES), jnp.bfloat16),
            pltpu.VMEM((2 * CELLS, DEPTH), jnp.bfloat16),
        ],
        compiler_params=pltpu.CompilerParams(vmem_limit_bytes=10 << 20),
        cost_estimate=pl.CostEstimate(
            flops=2 * ROWS * C * 2 * CELLS, bytes_accessed=3 << 20, transcendentals=4 * CELLS * CHANS
        ),
        name="norm_conv",
    )(sums, packed, tail, params, clips, weight)
    return lax.all_to_all(partial, "chan", 0, 0, tiled=True)


def on_device(
    clip_input, lengths, gamma_one, beta_one, w_one, bias_one, gamma_two, beta_two, w_two, bias_two
):
    count = lax.axis_size("tm")
    first = (lax.axis_index("tm") * 2).astype(jnp.int32).reshape(1)
    packed_shape = shape_of((CELLS, LANES), jnp.bfloat16)
    sums_shape = shape_of((count, 1, LANES), jnp.float32)
    flat_one = jnp.transpose(w_one, (1, 0, 2)).reshape(ROWS, C)
    flat_two = jnp.transpose(w_two, (1, 0, 2)).reshape(ROWS, C)
    packed, sums = pl.pallas_call(
        pack_kernel,
        out_shape=(packed_shape, sums_shape),
        in_specs=[HBM],
        out_specs=(VMEM, VMEM),
        scratch_shapes=[pltpu.VMEM((CHANS, 2, CELLS), jnp.bfloat16), pltpu.SemaphoreType.DMA],
        compiler_params=SMALL,
        name="pack",
    )(clip_input)
    everyone = lax.all_to_all(sums, "tm", 0, 0, tiled=True)
    tail = ring_shift(packed, "tm", 1)
    affine = (gamma_one, beta_one, bias_one, gamma_two, beta_two, bias_two, gamma_two, beta_two)
    params, clips = pl.pallas_call(
        prepare_kernel,
        out_shape=(shape_of((8, LANES), jnp.float32), shape_of((8, LANES), jnp.int32)),
        in_specs=[SMEM, SMEM, VMEM, VMEM, VMEM],
        out_specs=(VMEM, VMEM),
        compiler_params=SMALL,
        cost_estimate=pl.CostEstimate(flops=10000, bytes_accessed=2 << 20, transcendentals=0),
        name="prepare",
    )(lengths, first, packed, flat_one, jnp.stack(affine))
    parts = normed_conv(0, tail, packed, everyone, params, clips, flat_one)
    y_one, sums = pl.pallas_call(
        middle_kernel,
        out_shape=(packed_shape, sums_shape),
        in_specs=[VMEM, VMEM],
        out_specs=(VMEM, VMEM),
        compiler_params=SMALL,
        name="middle",
    )(parts, params)
    everyone = lax.all_to_all(sums, "tm", 0, 0, tiled=True)
    tail = ring_shift(y_one, "tm", 1)
    parts = normed_conv(3, tail, y_one, everyone, params, clips, flat_two)
    return pl.pallas_call(
        last_kernel,
        out_shape=shape_of(clip_input.shape, jnp.float32),
        in_specs=[VMEM, VMEM, VMEM],
        out_specs=VMEM,
        compiler_params=SMALL,
        name="last",
    )(parts, params, packed)


def solution(mesh):
    in_specs = (
        P("chan", "tm", None),
        P(),
        P("chan"),
        P("chan"),
        P("chan", None, None),
        P("chan"),
        P("chan"),
        P("chan"),
        P("chan", None, None),
        P("chan"),
    )
    out_specs = P("chan", "tm", None)
    return jax.shard_map(
        on_device, mesh=mesh, in_specs=in_specs, out_specs=out_specs, check_vma=False
    )
```

```python
import functools

import jax
import jax.numpy as jnp
from jax import lax
from jax.experimental import pallas as pl
from jax.experimental.pallas import tpu as pltpu
from jax.sharding import PartitionSpec as P

C = 512
GROUPS = 32
H = 16
W = 16
EPS = 1e-06
GROUP_SIZE = C // GROUPS
CELLS = H * W
CHANS = 64
LANES = 2 * CHANS
TAPS = 27
ROWS = TAPS * CHANS
DEPTH = (TAPS + 1) * CHANS
SLOT = CELLS + 2 * W

VMEM = pl.BlockSpec(memory_space=pltpu.VMEM)
SMEM = pl.BlockSpec(memory_space=pltpu.SMEM)
HBM = pl.BlockSpec(memory_space=pltpu.HBM)
SMALL = pltpu.CompilerParams(vmem_limit_bytes=4 << 20)


def ring_shift(value, axis, steps):
    count = lax.axis_size(axis)
    return lax.ppermute(value, axis, [(source, (source + steps) % count) for source in range(count)])


def left_half(shape):
    return lax.broadcasted_iota(jnp.int32, shape, len(shape) - 1) < CHANS


def group_totals(rows):
    lane = lax.broadcasted_iota(jnp.int32, rows.shape, 1)
    step = 1
    while step < GROUP_SIZE:
        other = jnp.where(
            (lane & step) == 0, pltpu.roll(rows, LANES - step, 1), pltpu.roll(rows, step, 1)
        )
        rows = rows + other
        step *= 2
    return rows


def holds_sum(shape):
    lane = lax.broadcasted_iota(jnp.int32, shape, len(shape) - 1)
    return (lane & (GROUP_SIZE // 2)) == 0


def write_sums(values, sums_ref):
    total = group_totals(jnp.sum(values, axis=0, keepdims=True))
    squares = group_totals(jnp.sum(values * values, axis=0, keepdims=True))
    row = jnp.where(holds_sum((1, LANES)), total, squares)
    sums_ref[...] = jnp.broadcast_to(row[None], sums_ref.shape)


def both_halves(row):
    return jnp.concatenate([row, row], axis=1)


def pack_kernel(x_hbm, packed_ref, sums_ref, x_ref, sem):
    load = pltpu.make_async_copy(x_hbm, x_ref, sem)
    load.start()
    load.wait()
    rows = jnp.concatenate([x_ref[:, 0, :], x_ref[:, 1, :]], axis=0).astype(jnp.float32)
    values = rows.T
    packed_ref[...] = values.astype(jnp.bfloat16)
    write_sums(values, sums_ref)


def clip_bounds(lengths_ref, frame):
    total = jnp.int32(0)
    start = jnp.int32(0)
    end = jnp.int32(0)
    for k in range(lengths_ref.shape[0]):
        after = total + lengths_ref[k]
        inside = (frame >= total) & (frame < after)
        start = jnp.where(inside, total, start)
        end = jnp.where(inside, after, end)
        total = after
    return start, end


def prepare_kernel(
    lengths_ref, first_ref, after_ref, weight_ref, affine_ref, params_ref, clips_ref
):
    del after_ref, weight_ref
    params_ref[...] = both_halves(affine_ref[...])
    frame = first_ref[0]
    start_zero, end_zero = clip_bounds(lengths_ref, frame)
    start_one, end_one = clip_bounds(lengths_ref, frame + 1)
    for k, number in enumerate((start_zero, end_zero, start_one, end_one, frame, frame, frame, frame)):
        clips_ref[k : k + 1, :] = jnp.full((1, LANES), number, jnp.int32)


def conv_kernel(
    at, sums_ref, own_ref, tail_ref, params_ref, clips_ref, w_ref, out_ref, slots_ref, cols_ref
):
    clips = clips_ref[...]
    start_zero, end_zero = clips[0:1, :], clips[1:2, :]
    start_one, end_one = clips[2:3, :], clips[3:4, :]
    frame = clips[4:5, :]
    count = sums_ref.shape[0]
    device = lax.broadcasted_iota(jnp.int32, (count, 1, LANES), 0)
    half = (lax.broadcasted_iota(jnp.int32, (count, 1, LANES), 2) >= CHANS).astype(jnp.int32)
    frame_of = 2 * device + half
    sums = sums_ref[:, 0:1, :]
    is_sum = holds_sum((1, LANES))
    stats = []
    for start, end in ((start_zero, end_zero), (start_one, end_one)):
        inside = (frame_of >= start[None]) & (frame_of < end[None])
        row = jnp.sum(jnp.where(inside, sums, 0.0), axis=0)
        size = ((end - start) * (GROUP_SIZE * CELLS)).astype(jnp.float32)
        row = (row + pltpu.roll(row, CHANS, 1)) / size
        mean = jnp.where(is_sum, row, pltpu.roll(row, GROUP_SIZE // 2, 1))
        second = jnp.where(is_sum, pltpu.roll(row, LANES - GROUP_SIZE // 2, 1), row)
        stats.append((mean, lax.rsqrt(second - mean * mean + EPS)))
    gamma = params_ref[at : at + 1, :]
    beta = params_ref[at + 1 : at + 2, :]
    left_row = left_half((1, LANES))
    mean_tail, scale_tail = stats[0]
    mean_own = jnp.where(left_row, stats[0][0], stats[1][0])
    scale_own = jnp.where(left_row, stats[0][1], stats[1][1])

    def normed(ref, mean, scale):
        u = (ref[...].astype(jnp.float32) - mean) * scale * gamma + beta
        return u / (1.0 + jnp.exp(-u))

    left = left_half((CELLS, LANES))

    def split(packed):
        turned = pltpu.roll(packed, CHANS, 1)
        return jnp.where(left, packed, turned), jnp.where(left, turned, packed)

    before_two, before_one = split(normed(tail_ref, mean_tail, scale_tail))
    own_zero, own_one = split(normed(own_ref, mean_own, scale_own))
    column = lax.broadcasted_iota(jnp.int32, (CELLS, LANES), 0) % W
    margin = jnp.zeros((W, LANES), jnp.bfloat16)

    def place(kw, slot, value):
        slots_ref[kw, slot, 0:W, :] = margin
        slots_ref[kw, slot, W : W + CELLS, :] = value
        slots_ref[kw, slot, W + CELLS :, :] = margin

    uses = (
        (before_two, ((0, frame - 2 >= start_zero),)),
        (before_one, ((1, frame - 1 >= start_zero), (3, frame - 1 >= start_one))),
        (own_zero, ((2, None), (4, frame >= start_one))),
        (own_one, ((5, None),)),
    )
    for value, targets in uses:
        views = (
            jnp.where(column == 0, 0.0, pltpu.roll(value, 1, 0)),
            value,
            jnp.where(column == W - 1, 0.0, pltpu.roll(value, CELLS - 1, 0)),
        )
        for kw, view in enumerate(views):
            for slot, kept in targets:
                shown = view if kept is None else jnp.where(kept, view, 0.0)
                place(kw, slot, shown.astype(jnp.bfloat16))

    def tap(own, index):
        kt, kh, kw = index // 9, (index // 3) % 3, index % 3
        return slots_ref[kw, 3 * own + kt, kh * W : kh * W + CELLS, :]

    for own in range(2):
        for pair in range(DEPTH // LANES):
            first = tap(own, 2 * pair)
            second = tap(own, 2 * pair + 1) if 2 * pair + 1 < TAPS else jnp.zeros_like(first)
            cols_ref[own * CELLS : (own + 1) * CELLS, pair * LANES : (pair + 1) * LANES] = jnp.where(
                left, first, second
            )
    for block in range(2):
        width = C // 2
        partial = jnp.dot(
            cols_ref[:, :ROWS],
            w_ref[:, block * width : (block + 1) * width],
            preferred_element_type=jnp.float32,
        )
        for tile in range(width // LANES):
            zero = partial[:CELLS, tile * LANES : (tile + 1) * LANES]
            one = partial[CELLS:, tile * LANES : (tile + 1) * LANES]
            place_at = block * (width // CHANS) + 2 * tile
            out_ref[place_at] = jnp.where(left, zero, pltpu.roll(one, CHANS, 1)).astype(jnp.bfloat16)
            out_ref[place_at + 1] = jnp.where(left, pltpu.roll(zero, CHANS, 1), one).astype(jnp.bfloat16)


def sum_partials(parts_ref, bias):
    total = parts_ref[0].astype(jnp.float32)
    for k in range(1, parts_ref.shape[0]):
        total = total + parts_ref[k].astype(jnp.float32)
    return total + bias


def middle_kernel(parts_ref, params_ref, y_ref, sums_ref):
    y = sum_partials(parts_ref, params_ref[2:3, :]).astype(jnp.bfloat16)
    y_ref[...] = y
    write_sums(y.astype(jnp.float32), sums_ref)


def last_kernel(parts_ref, params_ref, packed_ref, out_ref):
    value = sum_partials(parts_ref, params_ref[5:6, :]) + packed_ref[...].astype(jnp.float32)
    rows = value.T
    out_ref[:, 0, :] = rows[:CHANS]
    out_ref[:, 1, :] = rows[CHANS:]


def shape_of(shape, dtype):
    return jax.ShapeDtypeStruct(shape, dtype)


def normed_conv(at, tail, packed, sums, params, clips, weight):
    parts = C // CHANS
    partial = pl.pallas_call(
        functools.partial(conv_kernel, at),
        out_shape=shape_of((parts, CELLS, LANES), jnp.bfloat16),
        in_specs=[VMEM, VMEM, VMEM, VMEM, VMEM, VMEM],
        out_specs=VMEM,
        scratch_shapes=[
            pltpu.VMEM((3, 6, SLOT, LANES), jnp.bfloat16),
            pltpu.VMEM((2 * CELLS, DEPTH), jnp.bfloat16),
        ],
        compiler_params=pltpu.CompilerParams(vmem_limit_bytes=10 << 20),
        cost_estimate=pl.CostEstimate(
            flops=2 * ROWS * C * 2 * CELLS, bytes_accessed=3 << 20, transcendentals=4 * CELLS * CHANS
        ),
        name="norm_conv",
    )(sums, packed, tail, params, clips, weight)
    return lax.all_to_all(partial, "chan", 0, 0, tiled=True)


def on_device(
    clip_input, lengths, gamma_one, beta_one, w_one, bias_one, gamma_two, beta_two, w_two, bias_two
):
    count = lax.axis_size("tm")
    first = (lax.axis_index("tm") * 2).astype(jnp.int32).reshape(1)
    packed_shape = shape_of((CELLS, LANES), jnp.bfloat16)
    sums_shape = shape_of((count, 4, LANES), jnp.float32)
    flat_one = jnp.transpose(w_one, (1, 0, 2)).reshape(ROWS, C)
    flat_two = jnp.transpose(w_two, (1, 0, 2)).reshape(ROWS, C)
    packed, sums = pl.pallas_call(
        pack_kernel,
        out_shape=(packed_shape, sums_shape),
        in_specs=[HBM],
        out_specs=(VMEM, VMEM),
        scratch_shapes=[pltpu.VMEM((CHANS, 2, CELLS), jnp.bfloat16), pltpu.SemaphoreType.DMA],
        compiler_params=SMALL,
        name="pack",
    )(clip_input)
    tail = ring_shift(packed, "tm", 1)
    everyone = lax.all_to_all(sums, "tm", 0, 0, tiled=True)
    affine = (gamma_one, beta_one, bias_one, gamma_two, beta_two, bias_two, gamma_two, beta_two)
    params, clips = pl.pallas_call(
        prepare_kernel,
        out_shape=(shape_of((8, LANES), jnp.float32), shape_of((8, LANES), jnp.int32)),
        in_specs=[SMEM, SMEM, VMEM, VMEM, VMEM],
        out_specs=(VMEM, VMEM),
        compiler_params=SMALL,
        cost_estimate=pl.CostEstimate(flops=10000, bytes_accessed=2 << 20, transcendentals=0),
        name="prepare",
    )(lengths, first, packed, flat_one, jnp.stack(affine))
    parts = normed_conv(0, tail, packed, everyone, params, clips, flat_one)
    y_one, sums = pl.pallas_call(
        middle_kernel,
        out_shape=(packed_shape, sums_shape),
        in_specs=[VMEM, VMEM],
        out_specs=(VMEM, VMEM),
        compiler_params=SMALL,
        name="middle",
    )(parts, params)
    tail = ring_shift(y_one, "tm", 1)
    everyone = lax.all_to_all(sums, "tm", 0, 0, tiled=True)
    parts = normed_conv(3, tail, y_one, everyone, params, clips, flat_two)
    return pl.pallas_call(
        last_kernel,
        out_shape=shape_of(clip_input.shape, jnp.float32),
        in_specs=[VMEM, VMEM, VMEM],
        out_specs=VMEM,
        compiler_params=SMALL,
        name="last",
    )(parts, params, packed)


def solution(mesh):
    in_specs = (
        P("chan", "tm", None),
        P(),
        P("chan"),
        P("chan"),
        P("chan", None, None),
        P("chan"),
        P("chan"),
        P("chan"),
        P("chan", None, None),
        P("chan"),
    )
    out_specs = P("chan", "tm", None)
    return jax.shard_map(
        on_device, mesh=mesh, in_specs=in_specs, out_specs=out_specs, check_vma=False
    )
```

```python
import jax
import jax.numpy as jnp
from jax import lax
from jax.experimental import pallas as pl
from jax.experimental.pallas import tpu as pltpu
from jax.sharding import PartitionSpec as P

C = 512
GROUPS = 32
H = 16
W = 16
EPS = 1e-06
GROUP_SIZE = C // GROUPS
CELLS = H * W
CHANS = 64
LANES = 2 * CHANS
TAPS = 27
ROWS = TAPS * CHANS
DEPTH = (TAPS + 1) * CHANS
SLOT = CELLS + 2 * W

VMEM = pl.BlockSpec(memory_space=pltpu.VMEM)
SMEM = pl.BlockSpec(memory_space=pltpu.SMEM)
HBM = pl.BlockSpec(memory_space=pltpu.HBM)
SMALL = pltpu.CompilerParams(vmem_limit_bytes=4 << 20)


def ring_shift(value, axis, steps):
    count = lax.axis_size(axis)
    return lax.ppermute(value, axis, [(source, (source + steps) % count) for source in range(count)])


def left_half(shape):
    return lax.broadcasted_iota(jnp.int32, shape, len(shape) - 1) < CHANS


def group_totals(rows):
    lane = lax.broadcasted_iota(jnp.int32, rows.shape, 1)
    step = 1
    while step < GROUP_SIZE:
        other = jnp.where(
            (lane & step) == 0, pltpu.roll(rows, LANES - step, 1), pltpu.roll(rows, step, 1)
        )
        rows = rows + other
        step *= 2
    return rows


def holds_sum(shape):
    lane = lax.broadcasted_iota(jnp.int32, shape, len(shape) - 1)
    return (lane & (GROUP_SIZE // 2)) == 0


def write_sums(values, sums_ref):
    total = group_totals(jnp.sum(values, axis=0, keepdims=True))
    squares = group_totals(jnp.sum(values * values, axis=0, keepdims=True))
    row = jnp.where(holds_sum((1, LANES)), total, squares)
    sums_ref[...] = jnp.broadcast_to(row[None], sums_ref.shape)


def both_halves(row):
    return jnp.concatenate([row, row], axis=1)


def pack_kernel(x_hbm, packed_ref, sums_ref, x_ref, sem):
    load = pltpu.make_async_copy(x_hbm, x_ref, sem)
    load.start()
    load.wait()
    rows = jnp.concatenate([x_ref[:, 0, :], x_ref[:, 1, :]], axis=0).astype(jnp.float32)
    values = rows.T
    packed_ref[...] = values.astype(jnp.bfloat16)
    write_sums(values, sums_ref)


def clip_bounds(lengths_ref, frame):
    total = jnp.int32(0)
    start = jnp.int32(0)
    end = jnp.int32(0)
    for k in range(lengths_ref.shape[0]):
        after = total + lengths_ref[k]
        inside = (frame >= total) & (frame < after)
        start = jnp.where(inside, total, start)
        end = jnp.where(inside, after, end)
        total = after
    return start, end


def prepare_kernel(after_ref, weight_ref, affine_ref, params_ref):
    del after_ref, weight_ref
    params_ref[...] = both_halves(affine_ref[...])


def clips_kernel(lengths_ref, first_ref, after_ref, clips_ref):
    del after_ref
    frame = first_ref[0]
    start_zero, end_zero = clip_bounds(lengths_ref, frame)
    start_one, end_one = clip_bounds(lengths_ref, frame + 1)
    for k, number in enumerate((start_zero, end_zero, start_one, end_one, frame, frame, frame, frame)):
        clips_ref[k : k + 1, :] = jnp.full((1, LANES), number, jnp.int32)


def conv_kernel(
    sums_ref, own_ref, tail_ref, params_ref, clips_ref, w_ref, out_ref, slots_ref, cols_ref
):
    clips = clips_ref[...]
    start_zero, end_zero = clips[0:1, :], clips[1:2, :]
    start_one, end_one = clips[2:3, :], clips[3:4, :]
    frame = clips[4:5, :]
    count = sums_ref.shape[0]
    device = lax.broadcasted_iota(jnp.int32, (count, 1, LANES), 0)
    half = (lax.broadcasted_iota(jnp.int32, (count, 1, LANES), 2) >= CHANS).astype(jnp.int32)
    frame_of = 2 * device + half
    sums = sums_ref[:, 0:1, :]
    is_sum = holds_sum((1, LANES))
    stats = []
    for start, end in ((start_zero, end_zero), (start_one, end_one)):
        inside = (frame_of >= start[None]) & (frame_of < end[None])
        row = jnp.sum(jnp.where(inside, sums, 0.0), axis=0)
        size = ((end - start) * (GROUP_SIZE * CELLS)).astype(jnp.float32)
        row = (row + pltpu.roll(row, CHANS, 1)) / size
        mean = jnp.where(is_sum, row, pltpu.roll(row, GROUP_SIZE // 2, 1))
        second = jnp.where(is_sum, pltpu.roll(row, LANES - GROUP_SIZE // 2, 1), row)
        stats.append((mean, lax.rsqrt(second - mean * mean + EPS)))
    gamma = params_ref[0:1, :]
    beta = params_ref[1:2, :]
    left_row = left_half((1, LANES))
    mean_tail, scale_tail = stats[0]
    mean_own = jnp.where(left_row, stats[0][0], stats[1][0])
    scale_own = jnp.where(left_row, stats[0][1], stats[1][1])

    def normed(ref, mean, scale):
        u = (ref[...].astype(jnp.float32) - mean) * scale * gamma + beta
        return u / (1.0 + jnp.exp(-u))

    left = left_half((CELLS, LANES))

    def split(packed):
        turned = pltpu.roll(packed, CHANS, 1)
        return jnp.where(left, packed, turned), jnp.where(left, turned, packed)

    before_two, before_one = split(normed(tail_ref, mean_tail, scale_tail))
    own_zero, own_one = split(normed(own_ref, mean_own, scale_own))
    column = lax.broadcasted_iota(jnp.int32, (CELLS, LANES), 0) % W
    margin = jnp.zeros((W, LANES), jnp.bfloat16)

    def place(kw, slot, value):
        slots_ref[kw, slot, 0:W, :] = margin
        slots_ref[kw, slot, W : W + CELLS, :] = value
        slots_ref[kw, slot, W + CELLS :, :] = margin

    uses = (
        (before_two, ((0, frame - 2 >= start_zero),)),
        (before_one, ((1, frame - 1 >= start_zero), (3, frame - 1 >= start_one))),
        (own_zero, ((2, None), (4, frame >= start_one))),
        (own_one, ((5, None),)),
    )
    for value, targets in uses:
        views = (
            jnp.where(column == 0, 0.0, pltpu.roll(value, 1, 0)),
            value,
            jnp.where(column == W - 1, 0.0, pltpu.roll(value, CELLS - 1, 0)),
        )
        for kw, view in enumerate(views):
            for slot, kept in targets:
                shown = view if kept is None else jnp.where(kept, view, 0.0)
                place(kw, slot, shown.astype(jnp.bfloat16))

    def tap(own, index):
        kt, kh, kw = index // 9, (index // 3) % 3, index % 3
        return slots_ref[kw, 3 * own + kt, kh * W : kh * W + CELLS, :]

    for own in range(2):
        for pair in range(DEPTH // LANES):
            first = tap(own, 2 * pair)
            second = tap(own, 2 * pair + 1) if 2 * pair + 1 < TAPS else jnp.zeros_like(first)
            cols_ref[own * CELLS : (own + 1) * CELLS, pair * LANES : (pair + 1) * LANES] = jnp.where(
                left, first, second
            )
    for block in range(2):
        width = C // 2
        partial = jnp.dot(
            cols_ref[:, :ROWS],
            w_ref[:, block * width : (block + 1) * width],
            preferred_element_type=jnp.float32,
        )
        for tile in range(width // LANES):
            zero = partial[:CELLS, tile * LANES : (tile + 1) * LANES]
            one = partial[CELLS:, tile * LANES : (tile + 1) * LANES]
            place_at = block * (width // CHANS) + 2 * tile
            out_ref[place_at] = jnp.where(left, zero, pltpu.roll(one, CHANS, 1)).astype(jnp.bfloat16)
            out_ref[place_at + 1] = jnp.where(left, pltpu.roll(zero, CHANS, 1), one).astype(jnp.bfloat16)


def sum_partials(parts_ref, bias):
    total = parts_ref[0].astype(jnp.float32)
    for k in range(1, parts_ref.shape[0]):
        total = total + parts_ref[k].astype(jnp.float32)
    return total + bias


def middle_kernel(parts_ref, params_ref, y_ref, sums_ref):
    y = sum_partials(parts_ref, params_ref[2:3, :]).astype(jnp.bfloat16)
    y_ref[...] = y
    write_sums(y.astype(jnp.float32), sums_ref)


def last_kernel(parts_ref, params_ref, packed_ref, out_ref):
    value = sum_partials(parts_ref, params_ref[2:3, :]) + packed_ref[...].astype(jnp.float32)
    rows = value.T
    out_ref[:, 0, :] = rows[:CHANS]
    out_ref[:, 1, :] = rows[CHANS:]


def shape_of(shape, dtype):
    return jax.ShapeDtypeStruct(shape, dtype)


def prepare(after, weight, gamma, beta, bias):
    return pl.pallas_call(
        prepare_kernel,
        out_shape=shape_of((4, LANES), jnp.float32),
        in_specs=[VMEM, VMEM, VMEM],
        out_specs=VMEM,
        compiler_params=SMALL,
        cost_estimate=pl.CostEstimate(flops=10000, bytes_accessed=2 << 20, transcendentals=0),
        name="prepare",
    )(after, weight, jnp.stack((gamma, beta, bias, bias)))


def normed_conv(tail, packed, sums, params, clips, weight):
    parts = C // CHANS
    partial = pl.pallas_call(
        conv_kernel,
        out_shape=shape_of((parts, CELLS, LANES), jnp.bfloat16),
        in_specs=[VMEM, VMEM, VMEM, VMEM, VMEM, VMEM],
        out_specs=VMEM,
        scratch_shapes=[
            pltpu.VMEM((3, 6, SLOT, LANES), jnp.bfloat16),
            pltpu.VMEM((2 * CELLS, DEPTH), jnp.bfloat16),
        ],
        compiler_params=pltpu.CompilerParams(vmem_limit_bytes=10 << 20),
        cost_estimate=pl.CostEstimate(
            flops=2 * ROWS * C * 2 * CELLS, bytes_accessed=3 << 20, transcendentals=4 * CELLS * CHANS
        ),
        name="norm_conv",
    )(sums, packed, tail, params, clips, weight)
    return lax.all_to_all(partial, "chan", 0, 0, tiled=True)


def on_device(
    clip_input, lengths, gamma_one, beta_one, w_one, bias_one, gamma_two, beta_two, w_two, bias_two
):
    count = lax.axis_size("tm")
    first = (lax.axis_index("tm") * 2).astype(jnp.int32).reshape(1)
    packed_shape = shape_of((CELLS, LANES), jnp.bfloat16)
    sums_shape = shape_of((count, 4, LANES), jnp.float32)
    flat_one = jnp.transpose(w_one, (1, 0, 2)).reshape(ROWS, C)
    flat_two = jnp.transpose(w_two, (1, 0, 2)).reshape(ROWS, C)
    packed, sums = pl.pallas_call(
        pack_kernel,
        out_shape=(packed_shape, sums_shape),
        in_specs=[HBM],
        out_specs=(VMEM, VMEM),
        scratch_shapes=[pltpu.VMEM((CHANS, 2, CELLS), jnp.bfloat16), pltpu.SemaphoreType.DMA],
        compiler_params=SMALL,
        name="pack",
    )(clip_input)
    tail = ring_shift(packed, "tm", 1)
    everyone = lax.all_to_all(sums, "tm", 0, 0, tiled=True)
    clips = pl.pallas_call(
        clips_kernel,
        out_shape=shape_of((8, LANES), jnp.int32),
        in_specs=[SMEM, SMEM, VMEM],
        out_specs=VMEM,
        compiler_params=SMALL,
        cost_estimate=pl.CostEstimate(flops=10000, bytes_accessed=1 << 20, transcendentals=0),
        name="clips",
    )(lengths, first, packed)
    params = prepare(packed, flat_one, gamma_one, beta_one, bias_one)
    parts = normed_conv(tail, packed, everyone, params, clips, flat_one)
    y_one, sums = pl.pallas_call(
        middle_kernel,
        out_shape=(packed_shape, sums_shape),
        in_specs=[VMEM, VMEM],
        out_specs=(VMEM, VMEM),
        compiler_params=SMALL,
        name="middle",
    )(parts, params)
    tail = ring_shift(y_one, "tm", 1)
    everyone = lax.all_to_all(sums, "tm", 0, 0, tiled=True)
    params = prepare(y_one, flat_two, gamma_two, beta_two, bias_two)
    parts = normed_conv(tail, y_one, everyone, params, clips, flat_two)
    return pl.pallas_call(
        last_kernel,
        out_shape=shape_of(clip_input.shape, jnp.float32),
        in_specs=[VMEM, VMEM, VMEM],
        out_specs=VMEM,
        compiler_params=SMALL,
        name="last",
    )(parts, params, packed)


def solution(mesh):
    in_specs = (
        P("chan", "tm", None),
        P(),
        P("chan"),
        P("chan"),
        P("chan", None, None),
        P("chan"),
        P("chan"),
        P("chan"),
        P("chan", None, None),
        P("chan"),
    )
    out_specs = P("chan", "tm", None)
    return jax.shard_map(
        on_device, mesh=mesh, in_specs=in_specs, out_specs=out_specs, check_vma=False
    )
```

```python
import functools

import jax
import jax.numpy as jnp
from jax import lax
from jax.experimental import pallas as pl
from jax.experimental.pallas import tpu as pltpu
from jax.sharding import PartitionSpec as P

C = 512
GROUPS = 32
H = 16
W = 16
EPS = 1e-06
GROUP_SIZE = C // GROUPS
CELLS = H * W
CHANS = 64
LANES = 2 * CHANS
TAPS = 27
ROWS = TAPS * CHANS
DEPTH = (TAPS + 1) * CHANS
SLOT = CELLS + 2 * W

VMEM = pl.BlockSpec(memory_space=pltpu.VMEM)
SMEM = pl.BlockSpec(memory_space=pltpu.SMEM)
HBM = pl.BlockSpec(memory_space=pltpu.HBM)
SMALL = pltpu.CompilerParams(vmem_limit_bytes=4 << 20)


def in_hbm(value):
    return pltpu.with_memory_space_constraint(value, pltpu.HBM)


def ring_shift(value, axis, steps):
    count = lax.axis_size(axis)
    return lax.ppermute(value, axis, [(source, (source + steps) % count) for source in range(count)])


def left_half(shape):
    return lax.broadcasted_iota(jnp.int32, shape, len(shape) - 1) < CHANS


def group_totals(rows):
    lane = lax.broadcasted_iota(jnp.int32, rows.shape, 1)
    step = 1
    while step < GROUP_SIZE:
        other = jnp.where(
            (lane & step) == 0, pltpu.roll(rows, LANES - step, 1), pltpu.roll(rows, step, 1)
        )
        rows = rows + other
        step *= 2
    return rows


def holds_sum(shape):
    lane = lax.broadcasted_iota(jnp.int32, shape, len(shape) - 1)
    return (lane & (GROUP_SIZE // 2)) == 0


def write_sums(values, sums_ref):
    total = group_totals(jnp.sum(values, axis=0, keepdims=True))
    squares = group_totals(jnp.sum(values * values, axis=0, keepdims=True))
    row = jnp.where(holds_sum((1, LANES)), total, squares)
    sums_ref[...] = jnp.broadcast_to(row[None], sums_ref.shape)


def both_halves(row):
    return jnp.concatenate([row, row], axis=1)


def pack_kernel(x_hbm, packed_ref, sums_ref, x_ref, sem):
    load = pltpu.make_async_copy(x_hbm, x_ref, sem)
    load.start()
    load.wait()
    rows = jnp.concatenate([x_ref[:, 0, :], x_ref[:, 1, :]], axis=0).astype(jnp.float32)
    values = rows.T
    packed_ref[...] = values.astype(jnp.bfloat16)
    write_sums(values, sums_ref)


def clip_bounds(lengths_ref, frame):
    total = jnp.int32(0)
    start = jnp.int32(0)
    end = jnp.int32(0)
    for k in range(lengths_ref.shape[0]):
        after = total + lengths_ref[k]
        inside = (frame >= total) & (frame < after)
        start = jnp.where(inside, total, start)
        end = jnp.where(inside, after, end)
        total = after
    return start, end


def prepare_kernel(
    lengths_hbm, after_ref, gamma_one_hbm, beta_one_hbm, bias_one_hbm, gamma_two_hbm, beta_two_hbm,
    bias_two_hbm, params_ref, clips_ref, lengths_ref, rows_ref, sems,
):
    del after_ref
    affine = (gamma_one_hbm, beta_one_hbm, bias_one_hbm, gamma_two_hbm, beta_two_hbm, bias_two_hbm)
    loads = [pltpu.make_async_copy(lengths_hbm, lengths_ref, sems.at[len(affine)])]
    for k, ref in enumerate(affine):
        loads.append(pltpu.make_async_copy(ref, rows_ref.at[k], sems.at[k]))
    for load in loads:
        load.start()
    for load in loads:
        load.wait()
    for k in range(len(affine)):
        params_ref[k : k + 1, :] = both_halves(rows_ref[k])
    params_ref[len(affine) :, :] = jnp.zeros((8 - len(affine), LANES), jnp.float32)
    frame = (2 * lax.axis_index("tm")).astype(jnp.int32)
    start_zero, end_zero = clip_bounds(lengths_ref, frame)
    start_one, end_one = clip_bounds(lengths_ref, frame + 1)
    for k, number in enumerate((start_zero, end_zero, start_one, end_one, frame, frame, frame, frame)):
        clips_ref[k : k + 1, :] = jnp.full((1, LANES), number, jnp.int32)


def conv_kernel(
    at, sums_ref, own_ref, tail_ref, params_ref, clips_ref, w_hbm, out_ref, w_ref, slots_ref,
    cols_ref, sem,
):
    load = pltpu.make_async_copy(w_hbm, w_ref, sem)
    load.start()
    clips = clips_ref[...]
    start_zero, end_zero = clips[0:1, :], clips[1:2, :]
    start_one, end_one = clips[2:3, :], clips[3:4, :]
    frame = clips[4:5, :]
    count = sums_ref.shape[0]
    device = lax.broadcasted_iota(jnp.int32, (count, 1, LANES), 0)
    half = (lax.broadcasted_iota(jnp.int32, (count, 1, LANES), 2) >= CHANS).astype(jnp.int32)
    frame_of = 2 * device + half
    sums = sums_ref[:, 0:1, :]
    is_sum = holds_sum((1, LANES))
    stats = []
    for start, end in ((start_zero, end_zero), (start_one, end_one)):
        inside = (frame_of >= start[None]) & (frame_of < end[None])
        row = jnp.sum(jnp.where(inside, sums, 0.0), axis=0)
        size = ((end - start) * (GROUP_SIZE * CELLS)).astype(jnp.float32)
        row = (row + pltpu.roll(row, CHANS, 1)) / size
        mean = jnp.where(is_sum, row, pltpu.roll(row, GROUP_SIZE // 2, 1))
        second = jnp.where(is_sum, pltpu.roll(row, LANES - GROUP_SIZE // 2, 1), row)
        stats.append((mean, lax.rsqrt(second - mean * mean + EPS)))
    gamma = params_ref[at : at + 1, :]
    beta = params_ref[at + 1 : at + 2, :]
    left_row = left_half((1, LANES))
    mean_tail, scale_tail = stats[0]
    mean_own = jnp.where(left_row, stats[0][0], stats[1][0])
    scale_own = jnp.where(left_row, stats[0][1], stats[1][1])

    def normed(ref, mean, scale):
        u = (ref[...].astype(jnp.float32) - mean) * scale * gamma + beta
        return u / (1.0 + jnp.exp(-u))

    left = left_half((CELLS, LANES))

    def split(packed):
        turned = pltpu.roll(packed, CHANS, 1)
        return jnp.where(left, packed, turned), jnp.where(left, turned, packed)

    before_two, before_one = split(normed(tail_ref, mean_tail, scale_tail))
    own_zero, own_one = split(normed(own_ref, mean_own, scale_own))
    column = lax.broadcasted_iota(jnp.int32, (CELLS, LANES), 0) % W
    margin = jnp.zeros((W, LANES), jnp.bfloat16)

    def place(kw, slot, value):
        slots_ref[kw, slot, 0:W, :] = margin
        slots_ref[kw, slot, W : W + CELLS, :] = value
        slots_ref[kw, slot, W + CELLS :, :] = margin

    uses = (
        (before_two, ((0, frame - 2 >= start_zero),)),
        (before_one, ((1, frame - 1 >= start_zero), (3, frame - 1 >= start_one))),
        (own_zero, ((2, None), (4, frame >= start_one))),
        (own_one, ((5, None),)),
    )
    for value, targets in uses:
        views = (
            jnp.where(column == 0, 0.0, pltpu.roll(value, 1, 0)),
            value,
            jnp.where(column == W - 1, 0.0, pltpu.roll(value, CELLS - 1, 0)),
        )
        for kw, view in enumerate(views):
            for slot, kept in targets:
                shown = view if kept is None else jnp.where(kept, view, 0.0)
                place(kw, slot, shown.astype(jnp.bfloat16))

    def tap(own, index):
        kt, kh, kw = index // 9, (index // 3) % 3, index % 3
        return slots_ref[kw, 3 * own + kt, kh * W : kh * W + CELLS, :]

    for own in range(2):
        for pair in range(DEPTH // LANES):
            first = tap(own, 2 * pair)
            second = tap(own, 2 * pair + 1) if 2 * pair + 1 < TAPS else jnp.zeros_like(first)
            cols_ref[own * CELLS : (own + 1) * CELLS, pair * LANES : (pair + 1) * LANES] = jnp.where(
                left, first, second
            )
    load.wait()
    for block in range(2):
        width = C // 2
        partial = jnp.dot(
            cols_ref[:, :ROWS],
            w_ref[:, block * width : (block + 1) * width],
            preferred_element_type=jnp.float32,
        )
        for tile in range(width // LANES):
            zero = partial[:CELLS, tile * LANES : (tile + 1) * LANES]
            one = partial[CELLS:, tile * LANES : (tile + 1) * LANES]
            place_at = block * (width // CHANS) + 2 * tile
            out_ref[place_at] = jnp.where(left, zero, pltpu.roll(one, CHANS, 1)).astype(jnp.bfloat16)
            out_ref[place_at + 1] = jnp.where(left, pltpu.roll(zero, CHANS, 1), one).astype(jnp.bfloat16)


def sum_partials(parts_ref, bias):
    total = parts_ref[0].astype(jnp.float32)
    for k in range(1, parts_ref.shape[0]):
        total = total + parts_ref[k].astype(jnp.float32)
    return total + bias


def middle_kernel(parts_ref, params_ref, y_ref, sums_ref):
    y = sum_partials(parts_ref, params_ref[2:3, :]).astype(jnp.bfloat16)
    y_ref[...] = y
    write_sums(y.astype(jnp.float32), sums_ref)


def last_kernel(parts_ref, params_ref, packed_ref, out_ref):
    value = sum_partials(parts_ref, params_ref[5:6, :]) + packed_ref[...].astype(jnp.float32)
    rows = value.T
    out_ref[:, 0, :] = rows[:CHANS]
    out_ref[:, 1, :] = rows[CHANS:]


def shape_of(shape, dtype):
    return jax.ShapeDtypeStruct(shape, dtype)


def normed_conv(at, tail, packed, sums, params, clips, weight):
    parts = C // CHANS
    partial = pl.pallas_call(
        functools.partial(conv_kernel, at),
        out_shape=shape_of((parts, CELLS, LANES), jnp.bfloat16),
        in_specs=[VMEM, VMEM, VMEM, VMEM, VMEM, HBM],
        out_specs=VMEM,
        scratch_shapes=[
            pltpu.VMEM((ROWS, C), jnp.bfloat16),
            pltpu.VMEM((3, 6, SLOT, LANES), jnp.bfloat16),
            pltpu.VMEM((2 * CELLS, DEPTH), jnp.bfloat16),
            pltpu.SemaphoreType.DMA,
        ],
        compiler_params=pltpu.CompilerParams(vmem_limit_bytes=12 << 20),
        cost_estimate=pl.CostEstimate(
            flops=2 * ROWS * C * 2 * CELLS, bytes_accessed=3 << 20, transcendentals=4 * CELLS * CHANS
        ),
        name="norm_conv",
    )(sums, packed, tail, params, clips, weight)
    return lax.all_to_all(partial, "chan", 0, 0, tiled=True)


def on_device(
    clip_input, lengths, gamma_one, beta_one, w_one, bias_one, gamma_two, beta_two, w_two, bias_two
):
    count = lax.axis_size("tm")
    packed_shape = shape_of((CELLS, LANES), jnp.bfloat16)
    sums_shape = shape_of((count, 4, LANES), jnp.float32)
    flat_one = in_hbm(jnp.transpose(w_one, (1, 0, 2)).reshape(ROWS, C))
    flat_two = in_hbm(jnp.transpose(w_two, (1, 0, 2)).reshape(ROWS, C))
    packed, sums = pl.pallas_call(
        pack_kernel,
        out_shape=(packed_shape, sums_shape),
        in_specs=[HBM],
        out_specs=(VMEM, VMEM),
        scratch_shapes=[pltpu.VMEM((CHANS, 2, CELLS), jnp.bfloat16), pltpu.SemaphoreType.DMA],
        compiler_params=SMALL,
        name="pack",
    )(in_hbm(clip_input))
    tail = ring_shift(packed, "tm", 1)
    everyone = lax.all_to_all(sums, "tm", 0, 0, tiled=True)
    affine = (gamma_one, beta_one, bias_one, gamma_two, beta_two, bias_two)
    params, clips = pl.pallas_call(
        prepare_kernel,
        out_shape=(shape_of((8, LANES), jnp.float32), shape_of((8, LANES), jnp.int32)),
        in_specs=[HBM, VMEM] + [HBM] * len(affine),
        out_specs=(VMEM, VMEM),
        scratch_shapes=[
            pltpu.SMEM(lengths.shape, jnp.int32),
            pltpu.VMEM((len(affine), 1, CHANS), jnp.float32),
            pltpu.SemaphoreType.DMA((len(affine) + 1,)),
        ],
        compiler_params=SMALL,
        cost_estimate=pl.CostEstimate(flops=10000, bytes_accessed=1 << 20, transcendentals=0),
        name="prepare",
    )(in_hbm(lengths), packed, *[in_hbm(row.reshape(1, CHANS)) for row in affine])
    parts = normed_conv(0, tail, packed, everyone, params, clips, flat_one)
    y_one, sums = pl.pallas_call(
        middle_kernel,
        out_shape=(packed_shape, sums_shape),
        in_specs=[VMEM, VMEM],
        out_specs=(VMEM, VMEM),
        compiler_params=SMALL,
        name="middle",
    )(parts, params)
    tail = ring_shift(y_one, "tm", 1)
    everyone = lax.all_to_all(sums, "tm", 0, 0, tiled=True)
    parts = normed_conv(3, tail, y_one, everyone, params, clips, flat_two)
    return pl.pallas_call(
        last_kernel,
        out_shape=shape_of(clip_input.shape, jnp.float32),
        in_specs=[VMEM, VMEM, VMEM],
        out_specs=VMEM,
        compiler_params=SMALL,
        name="last",
    )(parts, params, packed)


def solution(mesh):
    in_specs = (
        P("chan", "tm", None),
        P(),
        P("chan"),
        P("chan"),
        P("chan", None, None),
        P("chan"),
        P("chan"),
        P("chan"),
        P("chan", None, None),
        P("chan"),
    )
    out_specs = P("chan", "tm", None)
    return jax.shard_map(
        on_device, mesh=mesh, in_specs=in_specs, out_specs=out_specs, check_vma=False
    )
```

```python
import functools

import jax
import jax.numpy as jnp
from jax import lax
from jax.experimental import pallas as pl
from jax.experimental.pallas import tpu as pltpu
from jax.sharding import PartitionSpec as P

C = 512
GROUPS = 32
H = 16
W = 16
EPS = 1e-06
GROUP_SIZE = C // GROUPS
CELLS = H * W
CHANS = 64
LANES = 2 * CHANS
TAPS = 27
ROWS = TAPS * CHANS
DEPTH = (TAPS + 1) * CHANS
SLOT = CELLS + 2 * W

VMEM = pl.BlockSpec(memory_space=pltpu.VMEM)
SMEM = pl.BlockSpec(memory_space=pltpu.SMEM)
HBM = pl.BlockSpec(memory_space=pltpu.HBM)
SMALL = pltpu.CompilerParams(vmem_limit_bytes=4 << 20)


def in_hbm(value):
    return pltpu.with_memory_space_constraint(value, pltpu.HBM)


def ring_shift(value, axis, steps):
    count = lax.axis_size(axis)
    return lax.ppermute(value, axis, [(source, (source + steps) % count) for source in range(count)])


def left_half(shape):
    return lax.broadcasted_iota(jnp.int32, shape, len(shape) - 1) < CHANS


def group_totals(rows):
    lane = lax.broadcasted_iota(jnp.int32, rows.shape, 1)
    step = 1
    while step < GROUP_SIZE:
        other = jnp.where(
            (lane & step) == 0, pltpu.roll(rows, LANES - step, 1), pltpu.roll(rows, step, 1)
        )
        rows = rows + other
        step *= 2
    return rows


def holds_sum(shape):
    lane = lax.broadcasted_iota(jnp.int32, shape, len(shape) - 1)
    return (lane & (GROUP_SIZE // 2)) == 0


def write_sums(values, sums_ref):
    total = group_totals(jnp.sum(values, axis=0, keepdims=True))
    squares = group_totals(jnp.sum(values * values, axis=0, keepdims=True))
    row = jnp.where(holds_sum((1, LANES)), total, squares)
    sums_ref[...] = jnp.broadcast_to(row[None], sums_ref.shape)


def both_halves(row):
    return jnp.concatenate([row, row], axis=1)


def pack_kernel(x_hbm, packed_ref, sums_ref, x_ref, sem):
    load = pltpu.make_async_copy(x_hbm, x_ref, sem)
    load.start()
    load.wait()
    rows = jnp.concatenate([x_ref[:, 0, :], x_ref[:, 1, :]], axis=0).astype(jnp.float32)
    values = rows.T
    packed_ref[...] = values.astype(jnp.bfloat16)
    write_sums(values, sums_ref)


def clip_bounds(lengths_ref, frame):
    total = jnp.int32(0)
    start = jnp.int32(0)
    end = jnp.int32(0)
    for k in range(lengths_ref.shape[0]):
        after = total + lengths_ref[k]
        inside = (frame >= total) & (frame < after)
        start = jnp.where(inside, total, start)
        end = jnp.where(inside, after, end)
        total = after
    return start, end


def prepare_kernel(
    lengths_hbm, after_ref, weight_ref, gamma_one_hbm, beta_one_hbm, bias_one_hbm, gamma_two_hbm, beta_two_hbm,
    bias_two_hbm, params_ref, clips_ref, lengths_ref, rows_ref, sems,
):
    del after_ref, weight_ref
    affine = (gamma_one_hbm, beta_one_hbm, bias_one_hbm, gamma_two_hbm, beta_two_hbm, bias_two_hbm)
    loads = [pltpu.make_async_copy(lengths_hbm, lengths_ref, sems.at[len(affine)])]
    for k, ref in enumerate(affine):
        loads.append(pltpu.make_async_copy(ref, rows_ref.at[k], sems.at[k]))
    for load in loads:
        load.start()
    for load in loads:
        load.wait()
    for k in range(len(affine)):
        params_ref[k : k + 1, :] = both_halves(rows_ref[k])
    params_ref[len(affine) :, :] = jnp.zeros((8 - len(affine), LANES), jnp.float32)
    frame = (2 * lax.axis_index("tm")).astype(jnp.int32)
    start_zero, end_zero = clip_bounds(lengths_ref, frame)
    start_one, end_one = clip_bounds(lengths_ref, frame + 1)
    for k, number in enumerate((start_zero, end_zero, start_one, end_one, frame, frame, frame, frame)):
        clips_ref[k : k + 1, :] = jnp.full((1, LANES), number, jnp.int32)


def fetch_kernel(weight_hbm, after_ref, weight_ref, sem):
    del after_ref
    load = pltpu.make_async_copy(weight_hbm, weight_ref, sem)
    load.start()
    load.wait()


def conv_kernel(
    at, sums_ref, own_ref, tail_ref, params_ref, clips_ref, w_ref, out_ref, slots_ref, cols_ref
):
    clips = clips_ref[...]
    start_zero, end_zero = clips[0:1, :], clips[1:2, :]
    start_one, end_one = clips[2:3, :], clips[3:4, :]
    frame = clips[4:5, :]
    count = sums_ref.shape[0]
    device = lax.broadcasted_iota(jnp.int32, (count, 1, LANES), 0)
    half = (lax.broadcasted_iota(jnp.int32, (count, 1, LANES), 2) >= CHANS).astype(jnp.int32)
    frame_of = 2 * device + half
    sums = sums_ref[:, 0:1, :]
    is_sum = holds_sum((1, LANES))
    stats = []
    for start, end in ((start_zero, end_zero), (start_one, end_one)):
        inside = (frame_of >= start[None]) & (frame_of < end[None])
        row = jnp.sum(jnp.where(inside, sums, 0.0), axis=0)
        size = ((end - start) * (GROUP_SIZE * CELLS)).astype(jnp.float32)
        row = (row + pltpu.roll(row, CHANS, 1)) / size
        mean = jnp.where(is_sum, row, pltpu.roll(row, GROUP_SIZE // 2, 1))
        second = jnp.where(is_sum, pltpu.roll(row, LANES - GROUP_SIZE // 2, 1), row)
        stats.append((mean, lax.rsqrt(second - mean * mean + EPS)))
    gamma = params_ref[at : at + 1, :]
    beta = params_ref[at + 1 : at + 2, :]
    left_row = left_half((1, LANES))
    mean_tail, scale_tail = stats[0]
    mean_own = jnp.where(left_row, stats[0][0], stats[1][0])
    scale_own = jnp.where(left_row, stats[0][1], stats[1][1])

    def normed(ref, mean, scale):
        u = (ref[...].astype(jnp.float32) - mean) * scale * gamma + beta
        return u / (1.0 + jnp.exp(-u))

    left = left_half((CELLS, LANES))

    def split(packed):
        turned = pltpu.roll(packed, CHANS, 1)
        return jnp.where(left, packed, turned), jnp.where(left, turned, packed)

    before_two, before_one = split(normed(tail_ref, mean_tail, scale_tail))
    own_zero, own_one = split(normed(own_ref, mean_own, scale_own))
    column = lax.broadcasted_iota(jnp.int32, (CELLS, LANES), 0) % W
    margin = jnp.zeros((W, LANES), jnp.bfloat16)

    def place(kw, slot, value):
        slots_ref[kw, slot, 0:W, :] = margin
        slots_ref[kw, slot, W : W + CELLS, :] = value
        slots_ref[kw, slot, W + CELLS :, :] = margin

    uses = (
        (before_two, ((0, frame - 2 >= start_zero),)),
        (before_one, ((1, frame - 1 >= start_zero), (3, frame - 1 >= start_one))),
        (own_zero, ((2, None), (4, frame >= start_one))),
        (own_one, ((5, None),)),
    )
    for value, targets in uses:
        views = (
            jnp.where(column == 0, 0.0, pltpu.roll(value, 1, 0)),
            value,
            jnp.where(column == W - 1, 0.0, pltpu.roll(value, CELLS - 1, 0)),
        )
        for kw, view in enumerate(views):
            for slot, kept in targets:
                shown = view if kept is None else jnp.where(kept, view, 0.0)
                place(kw, slot, shown.astype(jnp.bfloat16))

    def tap(own, index):
        kt, kh, kw = index // 9, (index // 3) % 3, index % 3
        return slots_ref[kw, 3 * own + kt, kh * W : kh * W + CELLS, :]

    for own in range(2):
        for pair in range(DEPTH // LANES):
            first = tap(own, 2 * pair)
            second = tap(own, 2 * pair + 1) if 2 * pair + 1 < TAPS else jnp.zeros_like(first)
            cols_ref[own * CELLS : (own + 1) * CELLS, pair * LANES : (pair + 1) * LANES] = jnp.where(
                left, first, second
            )
    for block in range(2):
        width = C // 2
        partial = jnp.dot(
            cols_ref[:, :ROWS],
            w_ref[:, block * width : (block + 1) * width],
            preferred_element_type=jnp.float32,
        )
        for tile in range(width // LANES):
            zero = partial[:CELLS, tile * LANES : (tile + 1) * LANES]
            one = partial[CELLS:, tile * LANES : (tile + 1) * LANES]
            place_at = block * (width // CHANS) + 2 * tile
            out_ref[place_at] = jnp.where(left, zero, pltpu.roll(one, CHANS, 1)).astype(jnp.bfloat16)
            out_ref[place_at + 1] = jnp.where(left, pltpu.roll(zero, CHANS, 1), one).astype(jnp.bfloat16)


def sum_partials(parts_ref, bias):
    total = parts_ref[0].astype(jnp.float32)
    for k in range(1, parts_ref.shape[0]):
        total = total + parts_ref[k].astype(jnp.float32)
    return total + bias


def middle_kernel(parts_ref, params_ref, y_ref, sums_ref):
    y = sum_partials(parts_ref, params_ref[2:3, :]).astype(jnp.bfloat16)
    y_ref[...] = y
    write_sums(y.astype(jnp.float32), sums_ref)


def last_kernel(parts_ref, params_ref, packed_ref, out_ref):
    value = sum_partials(parts_ref, params_ref[5:6, :]) + packed_ref[...].astype(jnp.float32)
    rows = value.T
    out_ref[:, 0, :] = rows[:CHANS]
    out_ref[:, 1, :] = rows[CHANS:]


def shape_of(shape, dtype):
    return jax.ShapeDtypeStruct(shape, dtype)


def normed_conv(at, tail, packed, sums, params, clips, weight):
    parts = C // CHANS
    partial = pl.pallas_call(
        functools.partial(conv_kernel, at),
        out_shape=shape_of((parts, CELLS, LANES), jnp.bfloat16),
        in_specs=[VMEM, VMEM, VMEM, VMEM, VMEM, VMEM],
        out_specs=VMEM,
        scratch_shapes=[
            pltpu.VMEM((3, 6, SLOT, LANES), jnp.bfloat16),
            pltpu.VMEM((2 * CELLS, DEPTH), jnp.bfloat16),
        ],
        compiler_params=pltpu.CompilerParams(vmem_limit_bytes=10 << 20),
        cost_estimate=pl.CostEstimate(
            flops=2 * ROWS * C * 2 * CELLS, bytes_accessed=3 << 20, transcendentals=4 * CELLS * CHANS
        ),
        name="norm_conv",
    )(sums, packed, tail, params, clips, weight)
    return lax.all_to_all(partial, "chan", 0, 0, tiled=True)


def on_device(
    clip_input, lengths, gamma_one, beta_one, w_one, bias_one, gamma_two, beta_two, w_two, bias_two
):
    count = lax.axis_size("tm")
    packed_shape = shape_of((CELLS, LANES), jnp.bfloat16)
    sums_shape = shape_of((count, 4, LANES), jnp.float32)
    flat_one = jnp.transpose(w_one, (1, 0, 2)).reshape(ROWS, C)
    flat_two = in_hbm(jnp.transpose(w_two, (1, 0, 2)).reshape(ROWS, C))
    packed, sums = pl.pallas_call(
        pack_kernel,
        out_shape=(packed_shape, sums_shape),
        in_specs=[HBM],
        out_specs=(VMEM, VMEM),
        scratch_shapes=[pltpu.VMEM((CHANS, 2, CELLS), jnp.bfloat16), pltpu.SemaphoreType.DMA],
        compiler_params=SMALL,
        name="pack",
    )(in_hbm(clip_input))
    tail = ring_shift(packed, "tm", 1)
    everyone = lax.all_to_all(sums, "tm", 0, 0, tiled=True)
    affine = (gamma_one, beta_one, bias_one, gamma_two, beta_two, bias_two)
    params, clips = pl.pallas_call(
        prepare_kernel,
        out_shape=(shape_of((8, LANES), jnp.float32), shape_of((8, LANES), jnp.int32)),
        in_specs=[HBM, VMEM, VMEM] + [HBM] * len(affine),
        out_specs=(VMEM, VMEM),
        scratch_shapes=[
            pltpu.SMEM(lengths.shape, jnp.int32),
            pltpu.VMEM((len(affine), 1, CHANS), jnp.float32),
            pltpu.SemaphoreType.DMA((len(affine) + 1,)),
        ],
        compiler_params=SMALL,
        cost_estimate=pl.CostEstimate(flops=10000, bytes_accessed=1 << 20, transcendentals=0),
        name="prepare",
    )(in_hbm(lengths), packed, flat_one, *[in_hbm(row.reshape(1, CHANS)) for row in affine])
    parts = normed_conv(0, tail, packed, everyone, params, clips, flat_one)
    y_one, sums = pl.pallas_call(
        middle_kernel,
        out_shape=(packed_shape, sums_shape),
        in_specs=[VMEM, VMEM],
        out_specs=(VMEM, VMEM),
        compiler_params=SMALL,
        name="middle",
    )(parts, params)
    tail = ring_shift(y_one, "tm", 1)
    everyone = lax.all_to_all(sums, "tm", 0, 0, tiled=True)
    held = pl.pallas_call(
        fetch_kernel,
        out_shape=shape_of((ROWS, C), jnp.bfloat16),
        in_specs=[HBM, VMEM],
        out_specs=VMEM,
        scratch_shapes=[pltpu.SemaphoreType.DMA],
        compiler_params=SMALL,
        cost_estimate=pl.CostEstimate(flops=10000, bytes_accessed=2 << 20, transcendentals=0),
        name="fetch",
    )(flat_two, y_one)
    parts = normed_conv(3, tail, y_one, everyone, params, clips, held)
    return pl.pallas_call(
        last_kernel,
        out_shape=shape_of(clip_input.shape, jnp.float32),
        in_specs=[VMEM, VMEM, VMEM],
        out_specs=VMEM,
        compiler_params=SMALL,
        name="last",
    )(parts, params, packed)


def solution(mesh):
    in_specs = (
        P("chan", "tm", None),
        P(),
        P("chan"),
        P("chan"),
        P("chan", None, None),
        P("chan"),
        P("chan"),
        P("chan"),
        P("chan", None, None),
        P("chan"),
    )
    out_specs = P("chan", "tm", None)
    return jax.shard_map(
        on_device, mesh=mesh, in_specs=in_specs, out_specs=out_specs, check_vma=False
    )
```

```python
import functools

import jax
import jax.numpy as jnp
from jax import lax
from jax.experimental import pallas as pl
from jax.experimental.pallas import tpu as pltpu
from jax.sharding import PartitionSpec as P

C = 512
GROUPS = 32
H = 16
W = 16
EPS = 1e-06
GROUP_SIZE = C // GROUPS
CELLS = H * W
CHANS = 64
LANES = 2 * CHANS
TAPS = 27
ROWS = TAPS * CHANS
DEPTH = (TAPS + 1) * CHANS
SLOT = CELLS + 2 * W

VMEM = pl.BlockSpec(memory_space=pltpu.VMEM)
SMEM = pl.BlockSpec(memory_space=pltpu.SMEM)
HBM = pl.BlockSpec(memory_space=pltpu.HBM)
SMALL = pltpu.CompilerParams(vmem_limit_bytes=4 << 20)


def in_hbm(value):
    return pltpu.with_memory_space_constraint(value, pltpu.HBM)


def ring_shift(value, axis, steps):
    count = lax.axis_size(axis)
    return lax.ppermute(value, axis, [(source, (source + steps) % count) for source in range(count)])


def left_half(shape):
    return lax.broadcasted_iota(jnp.int32, shape, len(shape) - 1) < CHANS


def group_totals(rows):
    lane = lax.broadcasted_iota(jnp.int32, rows.shape, 1)
    step = 1
    while step < GROUP_SIZE:
        other = jnp.where(
            (lane & step) == 0, pltpu.roll(rows, LANES - step, 1), pltpu.roll(rows, step, 1)
        )
        rows = rows + other
        step *= 2
    return rows


def holds_sum(shape):
    lane = lax.broadcasted_iota(jnp.int32, shape, len(shape) - 1)
    return (lane & (GROUP_SIZE // 2)) == 0


def write_sums(values, sums_ref):
    total = group_totals(jnp.sum(values, axis=0, keepdims=True))
    squares = group_totals(jnp.sum(values * values, axis=0, keepdims=True))
    row = jnp.where(holds_sum((1, LANES)), total, squares)
    sums_ref[...] = jnp.broadcast_to(row[None], sums_ref.shape)


def both_halves(row):
    return jnp.concatenate([row, row], axis=1)


def pack_kernel(x_hbm, packed_ref, sums_ref, x_ref, sem):
    load = pltpu.make_async_copy(x_hbm, x_ref, sem)
    load.start()
    load.wait()
    rows = jnp.concatenate([x_ref[:, 0, :], x_ref[:, 1, :]], axis=0).astype(jnp.float32)
    values = rows.T
    packed_ref[...] = values.astype(jnp.bfloat16)
    write_sums(values, sums_ref)


def clip_bounds(lengths_ref, frame):
    total = jnp.int32(0)
    start = jnp.int32(0)
    end = jnp.int32(0)
    for k in range(lengths_ref.shape[0]):
        after = total + lengths_ref[k]
        inside = (frame >= total) & (frame < after)
        start = jnp.where(inside, total, start)
        end = jnp.where(inside, after, end)
        total = after
    return start, end


def prepare_kernel(
    lengths_hbm, after_ref, gamma_one_hbm, beta_one_hbm, bias_one_hbm, gamma_two_hbm, beta_two_hbm,
    bias_two_hbm, params_ref, clips_ref, lengths_ref, rows_ref, sems,
):
    del after_ref
    affine = (gamma_one_hbm, beta_one_hbm, bias_one_hbm, gamma_two_hbm, beta_two_hbm, bias_two_hbm)
    loads = [pltpu.make_async_copy(lengths_hbm, lengths_ref, sems.at[len(affine)])]
    for k, ref in enumerate(affine):
        loads.append(pltpu.make_async_copy(ref, rows_ref.at[k], sems.at[k]))
    for load in loads:
        load.start()
    for load in loads:
        load.wait()
    for k in range(len(affine)):
        params_ref[k : k + 1, :] = both_halves(rows_ref[k])
    params_ref[len(affine) :, :] = jnp.zeros((8 - len(affine), LANES), jnp.float32)
    frame = (2 * lax.axis_index("tm")).astype(jnp.int32)
    start_zero, end_zero = clip_bounds(lengths_ref, frame)
    start_one, end_one = clip_bounds(lengths_ref, frame + 1)
    for k, number in enumerate((start_zero, end_zero, start_one, end_one, frame, frame, frame, frame)):
        clips_ref[k : k + 1, :] = jnp.full((1, LANES), number, jnp.int32)


def fetch_kernel(weight_hbm, after_ref, weight_ref, sem):
    del after_ref
    load = pltpu.make_async_copy(weight_hbm, weight_ref, sem)
    load.start()
    load.wait()


def conv_kernel(
    at, sums_ref, own_ref, tail_ref, params_ref, clips_ref, w_ref, out_ref, slots_ref, cols_ref
):
    clips = clips_ref[...]
    start_zero, end_zero = clips[0:1, :], clips[1:2, :]
    start_one, end_one = clips[2:3, :], clips[3:4, :]
    frame = clips[4:5, :]
    count = sums_ref.shape[0]
    device = lax.broadcasted_iota(jnp.int32, (count, 1, LANES), 0)
    half = (lax.broadcasted_iota(jnp.int32, (count, 1, LANES), 2) >= CHANS).astype(jnp.int32)
    frame_of = 2 * device + half
    sums = sums_ref[:, 0:1, :]
    is_sum = holds_sum((1, LANES))
    stats = []
    for start, end in ((start_zero, end_zero), (start_one, end_one)):
        inside = (frame_of >= start[None]) & (frame_of < end[None])
        row = jnp.sum(jnp.where(inside, sums, 0.0), axis=0)
        size = ((end - start) * (GROUP_SIZE * CELLS)).astype(jnp.float32)
        row = (row + pltpu.roll(row, CHANS, 1)) / size
        mean = jnp.where(is_sum, row, pltpu.roll(row, GROUP_SIZE // 2, 1))
        second = jnp.where(is_sum, pltpu.roll(row, LANES - GROUP_SIZE // 2, 1), row)
        stats.append((mean, lax.rsqrt(second - mean * mean + EPS)))
    gamma = params_ref[at : at + 1, :]
    beta = params_ref[at + 1 : at + 2, :]
    left_row = left_half((1, LANES))
    mean_tail, scale_tail = stats[0]
    mean_own = jnp.where(left_row, stats[0][0], stats[1][0])
    scale_own = jnp.where(left_row, stats[0][1], stats[1][1])

    def normed(ref, mean, scale):
        u = (ref[...].astype(jnp.float32) - mean) * scale * gamma + beta
        return u / (1.0 + jnp.exp(-u))

    left = left_half((CELLS, LANES))

    def split(packed):
        turned = pltpu.roll(packed, CHANS, 1)
        return jnp.where(left, packed, turned), jnp.where(left, turned, packed)

    before_two, before_one = split(normed(tail_ref, mean_tail, scale_tail))
    own_zero, own_one = split(normed(own_ref, mean_own, scale_own))
    column = lax.broadcasted_iota(jnp.int32, (CELLS, LANES), 0) % W
    margin = jnp.zeros((W, LANES), jnp.bfloat16)

    def place(kw, slot, value):
        slots_ref[kw, slot, 0:W, :] = margin
        slots_ref[kw, slot, W : W + CELLS, :] = value
        slots_ref[kw, slot, W + CELLS :, :] = margin

    uses = (
        (before_two, ((0, frame - 2 >= start_zero),)),
        (before_one, ((1, frame - 1 >= start_zero), (3, frame - 1 >= start_one))),
        (own_zero, ((2, None), (4, frame >= start_one))),
        (own_one, ((5, None),)),
    )
    for value, targets in uses:
        views = (
            jnp.where(column == 0, 0.0, pltpu.roll(value, 1, 0)),
            value,
            jnp.where(column == W - 1, 0.0, pltpu.roll(value, CELLS - 1, 0)),
        )
        for kw, view in enumerate(views):
            for slot, kept in targets:
                shown = view if kept is None else jnp.where(kept, view, 0.0)
                place(kw, slot, shown.astype(jnp.bfloat16))

    def tap(own, index):
        kt, kh, kw = index // 9, (index // 3) % 3, index % 3
        return slots_ref[kw, 3 * own + kt, kh * W : kh * W + CELLS, :]

    for own in range(2):
        for pair in range(DEPTH // LANES):
            first = tap(own, 2 * pair)
            second = tap(own, 2 * pair + 1) if 2 * pair + 1 < TAPS else jnp.zeros_like(first)
            cols_ref[own * CELLS : (own + 1) * CELLS, pair * LANES : (pair + 1) * LANES] = jnp.where(
                left, first, second
            )
    for block in range(2):
        width = C // 2
        partial = jnp.dot(
            cols_ref[:, :ROWS],
            w_ref[:, block * width : (block + 1) * width],
            preferred_element_type=jnp.float32,
        )
        for tile in range(width // LANES):
            zero = partial[:CELLS, tile * LANES : (tile + 1) * LANES]
            one = partial[CELLS:, tile * LANES : (tile + 1) * LANES]
            place_at = block * (width // CHANS) + 2 * tile
            out_ref[place_at] = jnp.where(left, zero, pltpu.roll(one, CHANS, 1)).astype(jnp.bfloat16)
            out_ref[place_at + 1] = jnp.where(left, pltpu.roll(zero, CHANS, 1), one).astype(jnp.bfloat16)


def sum_partials(parts_ref, bias):
    total = parts_ref[0].astype(jnp.float32)
    for k in range(1, parts_ref.shape[0]):
        total = total + parts_ref[k].astype(jnp.float32)
    return total + bias


def middle_kernel(parts_ref, params_ref, y_ref, sums_ref):
    y = sum_partials(parts_ref, params_ref[2:3, :]).astype(jnp.bfloat16)
    y_ref[...] = y
    write_sums(y.astype(jnp.float32), sums_ref)


def last_kernel(parts_ref, params_ref, packed_ref, out_ref):
    value = sum_partials(parts_ref, params_ref[5:6, :]) + packed_ref[...].astype(jnp.float32)
    rows = value.T
    out_ref[:, 0, :] = rows[:CHANS]
    out_ref[:, 1, :] = rows[CHANS:]


def shape_of(shape, dtype):
    return jax.ShapeDtypeStruct(shape, dtype)


def fetch(weight, after):
    return pl.pallas_call(
        fetch_kernel,
        out_shape=shape_of((ROWS, C), jnp.bfloat16),
        in_specs=[HBM, VMEM],
        out_specs=VMEM,
        scratch_shapes=[pltpu.SemaphoreType.DMA],
        compiler_params=SMALL,
        cost_estimate=pl.CostEstimate(flops=10000, bytes_accessed=2 << 20, transcendentals=0),
        name="fetch",
    )(weight, after)


def normed_conv(at, tail, packed, sums, params, clips, weight):
    parts = C // CHANS
    partial = pl.pallas_call(
        functools.partial(conv_kernel, at),
        out_shape=shape_of((parts, CELLS, LANES), jnp.bfloat16),
        in_specs=[VMEM, VMEM, VMEM, VMEM, VMEM, VMEM],
        out_specs=VMEM,
        scratch_shapes=[
            pltpu.VMEM((3, 6, SLOT, LANES), jnp.bfloat16),
            pltpu.VMEM((2 * CELLS, DEPTH), jnp.bfloat16),
        ],
        compiler_params=pltpu.CompilerParams(vmem_limit_bytes=10 << 20),
        cost_estimate=pl.CostEstimate(
            flops=2 * ROWS * C * 2 * CELLS, bytes_accessed=3 << 20, transcendentals=4 * CELLS * CHANS
        ),
        name="norm_conv",
    )(sums, packed, tail, params, clips, weight)
    return lax.all_to_all(partial, "chan", 0, 0, tiled=True)


def on_device(
    clip_input, lengths, gamma_one, beta_one, w_one, bias_one, gamma_two, beta_two, w_two, bias_two
):
    count = lax.axis_size("tm")
    packed_shape = shape_of((CELLS, LANES), jnp.bfloat16)
    sums_shape = shape_of((count, 4, LANES), jnp.float32)
    flat_one = in_hbm(jnp.transpose(w_one, (1, 0, 2)).reshape(ROWS, C))
    flat_two = in_hbm(jnp.transpose(w_two, (1, 0, 2)).reshape(ROWS, C))
    packed, sums = pl.pallas_call(
        pack_kernel,
        out_shape=(packed_shape, sums_shape),
        in_specs=[HBM],
        out_specs=(VMEM, VMEM),
        scratch_shapes=[pltpu.VMEM((CHANS, 2, CELLS), jnp.bfloat16), pltpu.SemaphoreType.DMA],
        compiler_params=SMALL,
        name="pack",
    )(in_hbm(clip_input))
    tail = ring_shift(packed, "tm", 1)
    everyone = lax.all_to_all(sums, "tm", 0, 0, tiled=True)
    affine = (gamma_one, beta_one, bias_one, gamma_two, beta_two, bias_two)
    params, clips = pl.pallas_call(
        prepare_kernel,
        out_shape=(shape_of((8, LANES), jnp.float32), shape_of((8, LANES), jnp.int32)),
        in_specs=[HBM, VMEM] + [HBM] * len(affine),
        out_specs=(VMEM, VMEM),
        scratch_shapes=[
            pltpu.SMEM(lengths.shape, jnp.int32),
            pltpu.VMEM((len(affine), 1, CHANS), jnp.float32),
            pltpu.SemaphoreType.DMA((len(affine) + 1,)),
        ],
        compiler_params=SMALL,
        cost_estimate=pl.CostEstimate(flops=10000, bytes_accessed=1 << 20, transcendentals=0),
        name="prepare",
    )(in_hbm(lengths), packed, *[in_hbm(row.reshape(1, CHANS)) for row in affine])
    parts = normed_conv(0, tail, packed, everyone, params, clips, fetch(flat_one, packed))
    y_one, sums = pl.pallas_call(
        middle_kernel,
        out_shape=(packed_shape, sums_shape),
        in_specs=[VMEM, VMEM],
        out_specs=(VMEM, VMEM),
        compiler_params=SMALL,
        name="middle",
    )(parts, params)
    tail = ring_shift(y_one, "tm", 1)
    everyone = lax.all_to_all(sums, "tm", 0, 0, tiled=True)
    held = fetch(flat_two, y_one)
    parts = normed_conv(3, tail, y_one, everyone, params, clips, held)
    return pl.pallas_call(
        last_kernel,
        out_shape=shape_of(clip_input.shape, jnp.float32),
        in_specs=[VMEM, VMEM, VMEM],
        out_specs=VMEM,
        compiler_params=SMALL,
        name="last",
    )(parts, params, packed)


def solution(mesh):
    in_specs = (
        P("chan", "tm", None),
        P(),
        P("chan"),
        P("chan"),
        P("chan", None, None),
        P("chan"),
        P("chan"),
        P("chan"),
        P("chan", None, None),
        P("chan"),
    )
    out_specs = P("chan", "tm", None)
    return jax.shard_map(
        on_device, mesh=mesh, in_specs=in_specs, out_specs=out_specs, check_vma=False
    )
```

```python
import functools

import jax
import jax.numpy as jnp
from jax import lax
from jax.experimental import pallas as pl
from jax.experimental.pallas import tpu as pltpu
from jax.sharding import PartitionSpec as P

C = 512
GROUPS = 32
H = 16
W = 16
EPS = 1e-06
GROUP_SIZE = C // GROUPS
CELLS = H * W
CHANS = 64
LANES = 2 * CHANS
TAPS = 27
ROWS = TAPS * CHANS
DEPTH = (TAPS + 1) * CHANS
SLOT = CELLS + 2 * W

VMEM = pl.BlockSpec(memory_space=pltpu.VMEM)
SMEM = pl.BlockSpec(memory_space=pltpu.SMEM)
HBM = pl.BlockSpec(memory_space=pltpu.HBM)
SMALL = pltpu.CompilerParams(vmem_limit_bytes=4 << 20)


def in_hbm(value):
    return pltpu.with_memory_space_constraint(value, pltpu.HBM)


def ring_shift(value, axis, steps):
    count = lax.axis_size(axis)
    return lax.ppermute(value, axis, [(source, (source + steps) % count) for source in range(count)])


def left_half(shape):
    return lax.broadcasted_iota(jnp.int32, shape, len(shape) - 1) < CHANS


def group_totals(rows):
    lane = lax.broadcasted_iota(jnp.int32, rows.shape, 1)
    step = 1
    while step < GROUP_SIZE:
        other = jnp.where(
            (lane & step) == 0, pltpu.roll(rows, LANES - step, 1), pltpu.roll(rows, step, 1)
        )
        rows = rows + other
        step *= 2
    return rows


def holds_sum(shape):
    lane = lax.broadcasted_iota(jnp.int32, shape, len(shape) - 1)
    return (lane & (GROUP_SIZE // 2)) == 0


def write_sums(values, sums_ref):
    total = group_totals(jnp.sum(values, axis=0, keepdims=True))
    squares = group_totals(jnp.sum(values * values, axis=0, keepdims=True))
    row = jnp.where(holds_sum((1, LANES)), total, squares)
    sums_ref[...] = jnp.broadcast_to(row[None], sums_ref.shape)


def both_halves(row):
    return jnp.concatenate([row, row], axis=1)


def clip_bounds(lengths_ref, frame):
    total = jnp.int32(0)
    start = jnp.int32(0)
    end = jnp.int32(0)
    for k in range(lengths_ref.shape[0]):
        after = total + lengths_ref[k]
        inside = (frame >= total) & (frame < after)
        start = jnp.where(inside, total, start)
        end = jnp.where(inside, after, end)
        total = after
    return start, end


def pack_kernel(
    x_hbm, lengths_hbm, gamma_one_hbm, beta_one_hbm, bias_one_hbm, gamma_two_hbm, beta_two_hbm,
    bias_two_hbm, packed_ref, sums_ref, params_ref, clips_ref, x_ref, lengths_ref, rows_ref, sems,
):
    affine = (gamma_one_hbm, beta_one_hbm, bias_one_hbm, gamma_two_hbm, beta_two_hbm, bias_two_hbm)
    large = pltpu.make_async_copy(x_hbm, x_ref, sems.at[len(affine) + 1])
    loads = [pltpu.make_async_copy(lengths_hbm, lengths_ref, sems.at[len(affine)])]
    for k, ref in enumerate(affine):
        loads.append(pltpu.make_async_copy(ref, rows_ref.at[k], sems.at[k]))
    large.start()
    for load in loads:
        load.start()
    for load in loads:
        load.wait()
    for k in range(len(affine)):
        params_ref[k : k + 1, :] = both_halves(rows_ref[k])
    params_ref[len(affine) :, :] = jnp.zeros((8 - len(affine), LANES), jnp.float32)
    frame = (2 * lax.axis_index("tm")).astype(jnp.int32)
    start_zero, end_zero = clip_bounds(lengths_ref, frame)
    start_one, end_one = clip_bounds(lengths_ref, frame + 1)
    for k, number in enumerate((start_zero, end_zero, start_one, end_one, frame, frame, frame, frame)):
        clips_ref[k : k + 1, :] = jnp.full((1, LANES), number, jnp.int32)
    large.wait()
    x = x_ref[...].astype(jnp.float32)
    values = jnp.concatenate([x[:, 0, :], x[:, 1, :]], axis=0).T
    packed_ref[...] = values.astype(jnp.bfloat16)
    write_sums(values, sums_ref)


def fetch_kernel(weight_hbm, after_ref, weight_ref, sem):
    del after_ref
    load = pltpu.make_async_copy(weight_hbm, weight_ref, sem)
    load.start()
    load.wait()


def conv_kernel(
    at, sums_ref, own_ref, tail_ref, params_ref, clips_ref, w_ref, out_ref, slots_ref, cols_ref
):
    clips = clips_ref[...]
    start_zero, end_zero = clips[0:1, :], clips[1:2, :]
    start_one, end_one = clips[2:3, :], clips[3:4, :]
    frame = clips[4:5, :]
    count = sums_ref.shape[0]
    device = lax.broadcasted_iota(jnp.int32, (count, 1, LANES), 0)
    half = (lax.broadcasted_iota(jnp.int32, (count, 1, LANES), 2) >= CHANS).astype(jnp.int32)
    frame_of = 2 * device + half
    sums = sums_ref[:, 0:1, :]
    is_sum = holds_sum((1, LANES))
    stats = []
    for start, end in ((start_zero, end_zero), (start_one, end_one)):
        inside = (frame_of >= start[None]) & (frame_of < end[None])
        row = jnp.sum(jnp.where(inside, sums, 0.0), axis=0)
        size = ((end - start) * (GROUP_SIZE * CELLS)).astype(jnp.float32)
        row = (row + pltpu.roll(row, CHANS, 1)) / size
        mean = jnp.where(is_sum, row, pltpu.roll(row, GROUP_SIZE // 2, 1))
        second = jnp.where(is_sum, pltpu.roll(row, LANES - GROUP_SIZE // 2, 1), row)
        stats.append((mean, lax.rsqrt(second - mean * mean + EPS)))
    gamma = params_ref[at : at + 1, :]
    beta = params_ref[at + 1 : at + 2, :]
    left_row = left_half((1, LANES))
    mean_tail, scale_tail = stats[0]
    mean_own = jnp.where(left_row, stats[0][0], stats[1][0])
    scale_own = jnp.where(left_row, stats[0][1], stats[1][1])

    def normed(ref, mean, scale):
        u = (ref[...].astype(jnp.float32) - mean) * scale * gamma + beta
        return u / (1.0 + jnp.exp(-u))

    left = left_half((CELLS, LANES))

    def split(packed):
        turned = pltpu.roll(packed, CHANS, 1)
        return jnp.where(left, packed, turned), jnp.where(left, turned, packed)

    before_two, before_one = split(normed(tail_ref, mean_tail, scale_tail))
    own_zero, own_one = split(normed(own_ref, mean_own, scale_own))
    column = lax.broadcasted_iota(jnp.int32, (CELLS, LANES), 0) % W
    margin = jnp.zeros((W, LANES), jnp.bfloat16)

    def place(kw, slot, value):
        slots_ref[kw, slot, 0:W, :] = margin
        slots_ref[kw, slot, W : W + CELLS, :] = value
        slots_ref[kw, slot, W + CELLS :, :] = margin

    uses = (
        (before_two, ((0, frame - 2 >= start_zero),)),
        (before_one, ((1, frame - 1 >= start_zero), (3, frame - 1 >= start_one))),
        (own_zero, ((2, None), (4, frame >= start_one))),
        (own_one, ((5, None),)),
    )
    for value, targets in uses:
        views = (
            jnp.where(column == 0, 0.0, pltpu.roll(value, 1, 0)),
            value,
            jnp.where(column == W - 1, 0.0, pltpu.roll(value, CELLS - 1, 0)),
        )
        for kw, view in enumerate(views):
            for slot, kept in targets:
                shown = view if kept is None else jnp.where(kept, view, 0.0)
                place(kw, slot, shown.astype(jnp.bfloat16))

    def tap(own, index):
        kt, kh, kw = index // 9, (index // 3) % 3, index % 3
        return slots_ref[kw, 3 * own + kt, kh * W : kh * W + CELLS, :]

    for own in range(2):
        for pair in range(DEPTH // LANES):
            first = tap(own, 2 * pair)
            second = tap(own, 2 * pair + 1) if 2 * pair + 1 < TAPS else jnp.zeros_like(first)
            cols_ref[own * CELLS : (own + 1) * CELLS, pair * LANES : (pair + 1) * LANES] = jnp.where(
                left, first, second
            )
    for block in range(2):
        width = C // 2
        partial = jnp.dot(
            cols_ref[:, :ROWS],
            w_ref[:, block * width : (block + 1) * width],
            preferred_element_type=jnp.float32,
        )
        for tile in range(width // LANES):
            zero = partial[:CELLS, tile * LANES : (tile + 1) * LANES]
            one = partial[CELLS:, tile * LANES : (tile + 1) * LANES]
            place_at = block * (width // CHANS) + 2 * tile
            out_ref[place_at] = jnp.where(left, zero, pltpu.roll(one, CHANS, 1)).astype(jnp.bfloat16)
            out_ref[place_at + 1] = jnp.where(left, pltpu.roll(zero, CHANS, 1), one).astype(jnp.bfloat16)


def sum_partials(parts_ref, bias):
    total = parts_ref[0].astype(jnp.float32)
    for k in range(1, parts_ref.shape[0]):
        total = total + parts_ref[k].astype(jnp.float32)
    return total + bias


def middle_kernel(parts_ref, params_ref, y_ref, sums_ref):
    y = sum_partials(parts_ref, params_ref[2:3, :]).astype(jnp.bfloat16)
    y_ref[...] = y
    write_sums(y.astype(jnp.float32), sums_ref)


def last_kernel(parts_ref, params_ref, packed_ref, out_ref):
    value = sum_partials(parts_ref, params_ref[5:6, :]) + packed_ref[...].astype(jnp.float32)
    rows = value.T
    out_ref[:, 0, :] = rows[:CHANS]
    out_ref[:, 1, :] = rows[CHANS:]


def shape_of(shape, dtype):
    return jax.ShapeDtypeStruct(shape, dtype)


def fetch(weight, after):
    return pl.pallas_call(
        fetch_kernel,
        out_shape=shape_of((ROWS, C), jnp.bfloat16),
        in_specs=[HBM, VMEM],
        out_specs=VMEM,
        scratch_shapes=[pltpu.SemaphoreType.DMA],
        compiler_params=SMALL,
        cost_estimate=pl.CostEstimate(flops=10000, bytes_accessed=2 << 20, transcendentals=0),
        name="fetch",
    )(weight, after)


def normed_conv(at, tail, packed, sums, params, clips, weight):
    parts = C // CHANS
    partial = pl.pallas_call(
        functools.partial(conv_kernel, at),
        out_shape=shape_of((parts, CELLS, LANES), jnp.bfloat16),
        in_specs=[VMEM, VMEM, VMEM, VMEM, VMEM, VMEM],
        out_specs=VMEM,
        scratch_shapes=[
            pltpu.VMEM((3, 6, SLOT, LANES), jnp.bfloat16),
            pltpu.VMEM((2 * CELLS, DEPTH), jnp.bfloat16),
        ],
        compiler_params=pltpu.CompilerParams(vmem_limit_bytes=10 << 20),
        cost_estimate=pl.CostEstimate(
            flops=2 * ROWS * C * 2 * CELLS, bytes_accessed=3 << 20, transcendentals=4 * CELLS * CHANS
        ),
        name="norm_conv",
    )(sums, packed, tail, params, clips, weight)
    return lax.all_to_all(partial, "chan", 0, 0, tiled=True)


def on_device(
    clip_input, lengths, gamma_one, beta_one, w_one, bias_one, gamma_two, beta_two, w_two, bias_two
):
    count = lax.axis_size("tm")
    packed_shape = shape_of((CELLS, LANES), jnp.bfloat16)
    sums_shape = shape_of((count, 4, LANES), jnp.float32)
    flat_one = in_hbm(jnp.transpose(w_one, (1, 0, 2)).reshape(ROWS, C))
    flat_two = in_hbm(jnp.transpose(w_two, (1, 0, 2)).reshape(ROWS, C))
    affine = (gamma_one, beta_one, bias_one, gamma_two, beta_two, bias_two)
    packed, sums, params, clips = pl.pallas_call(
        pack_kernel,
        out_shape=(
            packed_shape,
            sums_shape,
            shape_of((8, LANES), jnp.float32),
            shape_of((8, LANES), jnp.int32),
        ),
        in_specs=[HBM] * (2 + len(affine)),
        out_specs=(VMEM, VMEM, VMEM, VMEM),
        scratch_shapes=[
            pltpu.VMEM((CHANS, 2, CELLS), jnp.bfloat16),
            pltpu.SMEM(lengths.shape, jnp.int32),
            pltpu.VMEM((len(affine), 1, CHANS), jnp.float32),
            pltpu.SemaphoreType.DMA((len(affine) + 2,)),
        ],
        compiler_params=SMALL,
        name="pack",
    )(in_hbm(clip_input), in_hbm(lengths), *[in_hbm(row.reshape(1, CHANS)) for row in affine])
    tail = ring_shift(packed, "tm", 1)
    everyone = lax.all_to_all(sums, "tm", 0, 0, tiled=True)
    parts = normed_conv(0, tail, packed, everyone, params, clips, fetch(flat_one, packed))
    y_one, sums = pl.pallas_call(
        middle_kernel,
        out_shape=(packed_shape, sums_shape),
        in_specs=[VMEM, VMEM],
        out_specs=(VMEM, VMEM),
        compiler_params=SMALL,
        name="middle",
    )(parts, params)
    tail = ring_shift(y_one, "tm", 1)
    everyone = lax.all_to_all(sums, "tm", 0, 0, tiled=True)
    held = fetch(flat_two, y_one)
    parts = normed_conv(3, tail, y_one, everyone, params, clips, held)
    return pl.pallas_call(
        last_kernel,
        out_shape=shape_of(clip_input.shape, jnp.float32),
        in_specs=[VMEM, VMEM, VMEM],
        out_specs=VMEM,
        compiler_params=SMALL,
        name="last",
    )(parts, params, packed)


def solution(mesh):
    in_specs = (
        P("chan", "tm", None),
        P(),
        P("chan"),
        P("chan"),
        P("chan", None, None),
        P("chan"),
        P("chan"),
        P("chan"),
        P("chan", None, None),
        P("chan"),
    )
    out_specs = P("chan", "tm", None)
    return jax.shard_map(
        on_device, mesh=mesh, in_specs=in_specs, out_specs=out_specs, check_vma=False
    )
```

```python
import functools

import jax
import jax.numpy as jnp
from jax import lax
from jax.experimental import pallas as pl
from jax.experimental.pallas import tpu as pltpu
from jax.sharding import PartitionSpec as P

C = 512
GROUPS = 32
H = 16
W = 16
EPS = 1e-06
GROUP_SIZE = C // GROUPS
CELLS = H * W
CHANS = 64
LANES = 2 * CHANS
TAPS = 27
ROWS = TAPS * CHANS
DEPTH = (TAPS + 1) * CHANS
SLOT = CELLS + 2 * W

VMEM = pl.BlockSpec(memory_space=pltpu.VMEM)
SMEM = pl.BlockSpec(memory_space=pltpu.SMEM)
HBM = pl.BlockSpec(memory_space=pltpu.HBM)
SMALL = pltpu.CompilerParams(vmem_limit_bytes=4 << 20)


def in_hbm(value):
    return pltpu.with_memory_space_constraint(value, pltpu.HBM)


def ring_shift(value, axis, steps):
    count = lax.axis_size(axis)
    return lax.ppermute(value, axis, [(source, source + steps) for source in range(count - steps)])


def left_half(shape):
    return lax.broadcasted_iota(jnp.int32, shape, len(shape) - 1) < CHANS


def group_totals(rows):
    lane = lax.broadcasted_iota(jnp.int32, rows.shape, 1)
    step = 1
    while step < GROUP_SIZE:
        other = jnp.where(
            (lane & step) == 0, pltpu.roll(rows, LANES - step, 1), pltpu.roll(rows, step, 1)
        )
        rows = rows + other
        step *= 2
    return rows


def holds_sum(shape):
    lane = lax.broadcasted_iota(jnp.int32, shape, len(shape) - 1)
    return (lane & (GROUP_SIZE // 2)) == 0


def write_sums(values, sums_ref):
    total = group_totals(jnp.sum(values, axis=0, keepdims=True))
    squares = group_totals(jnp.sum(values * values, axis=0, keepdims=True))
    row = jnp.where(holds_sum((1, LANES)), total, squares)
    sums_ref[...] = jnp.broadcast_to(row[None], sums_ref.shape)


def both_halves(row):
    return jnp.concatenate([row, row], axis=1)


def pack_kernel(x_hbm, packed_ref, sums_ref, x_ref, sem):
    load = pltpu.make_async_copy(x_hbm, x_ref, sem)
    load.start()
    load.wait()
    rows = jnp.concatenate([x_ref[:, 0, :], x_ref[:, 1, :]], axis=0).astype(jnp.float32)
    values = rows.T
    packed_ref[...] = values.astype(jnp.bfloat16)
    write_sums(values, sums_ref)


def clip_bounds(lengths_ref, frame):
    total = jnp.int32(0)
    start = jnp.int32(0)
    end = jnp.int32(0)
    for k in range(lengths_ref.shape[0]):
        after = total + lengths_ref[k]
        inside = (frame >= total) & (frame < after)
        start = jnp.where(inside, total, start)
        end = jnp.where(inside, after, end)
        total = after
    return start, end


def prepare_kernel(
    lengths_hbm, after_ref, gamma_one_hbm, beta_one_hbm, bias_one_hbm, gamma_two_hbm, beta_two_hbm,
    bias_two_hbm, params_ref, clips_ref, lengths_ref, rows_ref, sems,
):
    del after_ref
    affine = (gamma_one_hbm, beta_one_hbm, bias_one_hbm, gamma_two_hbm, beta_two_hbm, bias_two_hbm)
    loads = [pltpu.make_async_copy(lengths_hbm, lengths_ref, sems.at[len(affine)])]
    for k, ref in enumerate(affine):
        loads.append(pltpu.make_async_copy(ref, rows_ref.at[k], sems.at[k]))
    for load in loads:
        load.start()
    for load in loads:
        load.wait()
    for k in range(len(affine)):
        params_ref[k : k + 1, :] = both_halves(rows_ref[k])
    params_ref[len(affine) :, :] = jnp.zeros((8 - len(affine), LANES), jnp.float32)
    frame = (2 * lax.axis_index("tm")).astype(jnp.int32)
    start_zero, end_zero = clip_bounds(lengths_ref, frame)
    start_one, end_one = clip_bounds(lengths_ref, frame + 1)
    for k, number in enumerate((start_zero, end_zero, start_one, end_one, frame, frame, frame, frame)):
        clips_ref[k : k + 1, :] = jnp.full((1, LANES), number, jnp.int32)


def fetch_kernel(weight_hbm, after_ref, weight_ref, sem):
    del after_ref
    load = pltpu.make_async_copy(weight_hbm, weight_ref, sem)
    load.start()
    load.wait()


def conv_kernel(
    at, sums_ref, own_ref, tail_ref, params_ref, clips_ref, w_ref, out_ref, slots_ref, cols_ref
):
    clips = clips_ref[...]
    start_zero, end_zero = clips[0:1, :], clips[1:2, :]
    start_one, end_one = clips[2:3, :], clips[3:4, :]
    frame = clips[4:5, :]
    count = sums_ref.shape[0]
    device = lax.broadcasted_iota(jnp.int32, (count, 1, LANES), 0)
    half = (lax.broadcasted_iota(jnp.int32, (count, 1, LANES), 2) >= CHANS).astype(jnp.int32)
    frame_of = 2 * device + half
    sums = sums_ref[:, 0:1, :]
    is_sum = holds_sum((1, LANES))
    stats = []
    for start, end in ((start_zero, end_zero), (start_one, end_one)):
        inside = (frame_of >= start[None]) & (frame_of < end[None])
        row = jnp.sum(jnp.where(inside, sums, 0.0), axis=0)
        size = ((end - start) * (GROUP_SIZE * CELLS)).astype(jnp.float32)
        row = (row + pltpu.roll(row, CHANS, 1)) / size
        mean = jnp.where(is_sum, row, pltpu.roll(row, GROUP_SIZE // 2, 1))
        second = jnp.where(is_sum, pltpu.roll(row, LANES - GROUP_SIZE // 2, 1), row)
        stats.append((mean, lax.rsqrt(second - mean * mean + EPS)))
    gamma = params_ref[at : at + 1, :]
    beta = params_ref[at + 1 : at + 2, :]
    left_row = left_half((1, LANES))
    mean_tail, scale_tail = stats[0]
    mean_own = jnp.where(left_row, stats[0][0], stats[1][0])
    scale_own = jnp.where(left_row, stats[0][1], stats[1][1])

    def normed(ref, mean, scale):
        u = (ref[...].astype(jnp.float32) - mean) * scale * gamma + beta
        return u / (1.0 + jnp.exp(-u))

    left = left_half((CELLS, LANES))

    def split(packed):
        turned = pltpu.roll(packed, CHANS, 1)
        return jnp.where(left, packed, turned), jnp.where(left, turned, packed)

    before_two, before_one = split(normed(tail_ref, mean_tail, scale_tail))
    own_zero, own_one = split(normed(own_ref, mean_own, scale_own))
    column = lax.broadcasted_iota(jnp.int32, (CELLS, LANES), 0) % W
    margin = jnp.zeros((W, LANES), jnp.bfloat16)

    def place(kw, slot, value):
        slots_ref[kw, slot, 0:W, :] = margin
        slots_ref[kw, slot, W : W + CELLS, :] = value
        slots_ref[kw, slot, W + CELLS :, :] = margin

    uses = (
        (before_two, ((0, frame - 2 >= start_zero),)),
        (before_one, ((1, frame - 1 >= start_zero), (3, frame - 1 >= start_one))),
        (own_zero, ((2, None), (4, frame >= start_one))),
        (own_one, ((5, None),)),
    )
    for value, targets in uses:
        views = (
            jnp.where(column == 0, 0.0, pltpu.roll(value, 1, 0)),
            value,
            jnp.where(column == W - 1, 0.0, pltpu.roll(value, CELLS - 1, 0)),
        )
        for kw, view in enumerate(views):
            for slot, kept in targets:
                shown = view if kept is None else jnp.where(kept, view, 0.0)
                place(kw, slot, shown.astype(jnp.bfloat16))

    def tap(own, index):
        kt, kh, kw = index // 9, (index // 3) % 3, index % 3
        return slots_ref[kw, 3 * own + kt, kh * W : kh * W + CELLS, :]

    for own in range(2):
        for pair in range(DEPTH // LANES):
            first = tap(own, 2 * pair)
            second = tap(own, 2 * pair + 1) if 2 * pair + 1 < TAPS else jnp.zeros_like(first)
            cols_ref[own * CELLS : (own + 1) * CELLS, pair * LANES : (pair + 1) * LANES] = jnp.where(
                left, first, second
            )
    for block in range(2):
        width = C // 2
        partial = jnp.dot(
            cols_ref[:, :ROWS],
            w_ref[:, block * width : (block + 1) * width],
            preferred_element_type=jnp.float32,
        )
        for tile in range(width // LANES):
            zero = partial[:CELLS, tile * LANES : (tile + 1) * LANES]
            one = partial[CELLS:, tile * LANES : (tile + 1) * LANES]
            place_at = block * (width // CHANS) + 2 * tile
            out_ref[place_at] = jnp.where(left, zero, pltpu.roll(one, CHANS, 1)).astype(jnp.bfloat16)
            out_ref[place_at + 1] = jnp.where(left, pltpu.roll(zero, CHANS, 1), one).astype(jnp.bfloat16)


def sum_partials(parts_ref, bias):
    total = parts_ref[0].astype(jnp.float32)
    for k in range(1, parts_ref.shape[0]):
        total = total + parts_ref[k].astype(jnp.float32)
    return total + bias


def middle_kernel(parts_ref, params_ref, y_ref, sums_ref):
    y = sum_partials(parts_ref, params_ref[2:3, :]).astype(jnp.bfloat16)
    y_ref[...] = y
    write_sums(y.astype(jnp.float32), sums_ref)


def last_kernel(parts_ref, params_ref, packed_ref, out_ref):
    value = sum_partials(parts_ref, params_ref[5:6, :]) + packed_ref[...].astype(jnp.float32)
    rows = value.T
    out_ref[:, 0, :] = rows[:CHANS]
    out_ref[:, 1, :] = rows[CHANS:]


def shape_of(shape, dtype):
    return jax.ShapeDtypeStruct(shape, dtype)


def fetch(weight, after):
    return pl.pallas_call(
        fetch_kernel,
        out_shape=shape_of((ROWS, C), jnp.bfloat16),
        in_specs=[HBM, VMEM],
        out_specs=VMEM,
        scratch_shapes=[pltpu.SemaphoreType.DMA],
        compiler_params=SMALL,
        cost_estimate=pl.CostEstimate(flops=10000, bytes_accessed=2 << 20, transcendentals=0),
        name="fetch",
    )(weight, after)


def normed_conv(at, tail, packed, sums, params, clips, weight):
    parts = C // CHANS
    partial = pl.pallas_call(
        functools.partial(conv_kernel, at),
        out_shape=shape_of((parts, CELLS, LANES), jnp.bfloat16),
        in_specs=[VMEM, VMEM, VMEM, VMEM, VMEM, VMEM],
        out_specs=VMEM,
        scratch_shapes=[
            pltpu.VMEM((3, 6, SLOT, LANES), jnp.bfloat16),
            pltpu.VMEM((2 * CELLS, DEPTH), jnp.bfloat16),
        ],
        compiler_params=pltpu.CompilerParams(vmem_limit_bytes=10 << 20),
        cost_estimate=pl.CostEstimate(
            flops=2 * ROWS * C * 2 * CELLS, bytes_accessed=3 << 20, transcendentals=4 * CELLS * CHANS
        ),
        name="norm_conv",
    )(sums, packed, tail, params, clips, weight)
    return lax.all_to_all(partial, "chan", 0, 0, tiled=True)


def on_device(
    clip_input, lengths, gamma_one, beta_one, w_one, bias_one, gamma_two, beta_two, w_two, bias_two
):
    count = lax.axis_size("tm")
    packed_shape = shape_of((CELLS, LANES), jnp.bfloat16)
    sums_shape = shape_of((count, 4, LANES), jnp.float32)
    flat_one = in_hbm(jnp.transpose(w_one, (1, 0, 2)).reshape(ROWS, C))
    flat_two = in_hbm(jnp.transpose(w_two, (1, 0, 2)).reshape(ROWS, C))
    packed, sums = pl.pallas_call(
        pack_kernel,
        out_shape=(packed_shape, sums_shape),
        in_specs=[HBM],
        out_specs=(VMEM, VMEM),
        scratch_shapes=[pltpu.VMEM((CHANS, 2, CELLS), jnp.bfloat16), pltpu.SemaphoreType.DMA],
        compiler_params=SMALL,
        name="pack",
    )(in_hbm(clip_input))
    tail = ring_shift(packed, "tm", 1)
    everyone = lax.all_to_all(sums, "tm", 0, 0, tiled=True)
    affine = (gamma_one, beta_one, bias_one, gamma_two, beta_two, bias_two)
    params, clips = pl.pallas_call(
        prepare_kernel,
        out_shape=(shape_of((8, LANES), jnp.float32), shape_of((8, LANES), jnp.int32)),
        in_specs=[HBM, VMEM] + [HBM] * len(affine),
        out_specs=(VMEM, VMEM),
        scratch_shapes=[
            pltpu.SMEM(lengths.shape, jnp.int32),
            pltpu.VMEM((len(affine), 1, CHANS), jnp.float32),
            pltpu.SemaphoreType.DMA((len(affine) + 1,)),
        ],
        compiler_params=SMALL,
        cost_estimate=pl.CostEstimate(flops=10000, bytes_accessed=1 << 20, transcendentals=0),
        name="prepare",
    )(in_hbm(lengths), packed, *[in_hbm(row.reshape(1, CHANS)) for row in affine])
    parts = normed_conv(0, tail, packed, everyone, params, clips, fetch(flat_one, packed))
    y_one, sums = pl.pallas_call(
        middle_kernel,
        out_shape=(packed_shape, sums_shape),
        in_specs=[VMEM, VMEM],
        out_specs=(VMEM, VMEM),
        compiler_params=SMALL,
        name="middle",
    )(parts, params)
    tail = ring_shift(y_one, "tm", 1)
    everyone = lax.all_to_all(sums, "tm", 0, 0, tiled=True)
    held = fetch(flat_two, y_one)
    parts = normed_conv(3, tail, y_one, everyone, params, clips, held)
    return pl.pallas_call(
        last_kernel,
        out_shape=shape_of(clip_input.shape, jnp.float32),
        in_specs=[VMEM, VMEM, VMEM],
        out_specs=VMEM,
        compiler_params=SMALL,
        name="last",
    )(parts, params, packed)


def solution(mesh):
    in_specs = (
        P("chan", "tm", None),
        P(),
        P("chan"),
        P("chan"),
        P("chan", None, None),
        P("chan"),
        P("chan"),
        P("chan"),
        P("chan", None, None),
        P("chan"),
    )
    out_specs = P("chan", "tm", None)
    return jax.shard_map(
        on_device, mesh=mesh, in_specs=in_specs, out_specs=out_specs, check_vma=False
    )
```
